32 devices in a mesh: crops: 2 (over y), rows: 4 (over z), chan: 2 (over x), sub: 2 (over core).
Axes of the slice: x: 2, y: 2, z: 4, core: 2. Of those that a mesh axis runs over, the one named last changes fastest.
Arguments:
- pair: bfloat16 [64, 32, 128], P(('crops', 'rows', 'sub')), parts along dimension 0, may hold values from -6 to 6
- residue_mask: int32 [64], P('crops'), parts along dimension 0, may hold values from 0 to 1, as said below
- in_gain: float32 [2, 128], replicated, may hold values from 0.1 to 1.9
- in_bias: float32 [2, 128], replicated, may hold values from -3 to 3
- projections: bfloat16 [2, 4, 128, 128], P(None, None, None, 'chan'), may hold values from -0.5 to 0.5
- gate_weight: bfloat16 [2, 128, 128], replicated, may hold values from -0.5 to 0.5
- out_gain: float32 [2, 128], replicated, may hold values from 0.1 to 1.9
- out_bias: float32 [2, 128], replicated, may hold values from -3 to 3
- out_weight: bfloat16 [2, 128, 128], replicated, may hold values from -0.5 to 0.5
Outputs:
- pair_out: bfloat16 [64, 32, 128], P(('crops', 'rows', 'sub'), 'chan'), parts along dimension 0
The draws below stay inside these ranges and needn't reach their ends.
There are 2 independent parts, one for each index of `crops`. The reference program is written for one: setup_inputs(seed, part) draws one part's arguments, and reference() takes and returns one part's arrays. A program takes and returns all parts, laid end to end along the dimension named above; an argument that names none is the same for every part. Nothing has to cross between parts.
Inputs may be any that keep to these rules, and one draw needn't show every extreme that they name: `residue_mask`: residue 0 is always present and residue 32 - 1 is always a gap or padding.
All inputs are finite; a program needn't handle non-finite values.
Results may differ from the reference program's by a relative error of at most 0.012.
Values may be sent and summed in bfloat16 or wider, within the bound.
A program may use at most 64 MiB of HBM per device.

```python
import jax
import jax.numpy as jnp
from jax import lax

C = 128
H = 128
N = 32


def draw_residue_mask(key, part):
    levels = jax.random.randint(jax.random.fold_in(key, 7), (N,), 0, 4)
    present = (levels != 0).astype(jnp.int32)
    positions = jnp.arange(N)
    present = jnp.where(positions == 0, 1, present)
    present = jnp.where(positions == N - 1, 0, present)
    return present.astype(jnp.int32)


def shard_levels(stream_key, shape, shards, smallest, largest):
    def one(dim, blocks):
        steps = jax.random.uniform(jax.random.fold_in(jax.random.fold_in(stream_key, 6), dim), (blocks,), jnp.float32, smallest / len(shards), largest / len(shards))
        return jnp.repeat(jnp.exp(steps), shape[dim] // blocks).reshape((-1,) + (1,) * (len(shape) - dim - 1))

    loudness = one(*shards[0])
    for cut in shards[1:]:
        loudness = loudness * one(*cut)
    return loudness


def normal_values(rng, shape, scale, most, pieces=(), dtype=jnp.bfloat16):
    result = jax.random.normal(rng, shape, jnp.float32) * scale
    if len(pieces) > 0:
        result = shard_levels(rng, shape, pieces, -0.22, 0.18) * result
    return jnp.clip(result, min=-most, max=most).astype(dtype)


def setup_inputs(seed: int = 0, part: int = 0) -> dict:
    key_of = jax.random.split(jax.random.key(seed), 10)
    part_splits = jax.random.split(jax.random.fold_in(key_of[9], part), 10)
    return {
        "pair": normal_values(part_splits[0], (N, N, C), 1.0, 6.0, ((0, 8),)),
        "residue_mask": draw_residue_mask(jax.random.fold_in(jax.random.fold_in(key_of[9], part), 71), part),
        "in_gain": jnp.clip(1.0 + 0.18 * jax.random.normal(key_of[2], (2, C), jnp.float32), 0.1, 1.9),
        "in_bias": normal_values(key_of[3], (2, C), 0.5, 3.0, (), jnp.float32),
        "projections": normal_values(key_of[4], (2, 4, C, H), C ** -0.5, 0.5, ((3, 2),)),
        "gate_weight": normal_values(key_of[5], (2, C, C), C ** -0.5, 0.5),
        "out_gain": jnp.clip(1.0 + 0.18 * jax.random.normal(key_of[6], (2, H), jnp.float32), 0.1, 1.9),
        "out_bias": normal_values(key_of[7], (2, H), 0.5, 3.0, (), jnp.float32),
        "out_weight": normal_values(key_of[8], (2, H, C), H ** -0.5, 0.5),
    }


epsilon = 1e-05

def normalize(values, reduce_axis):
    centre = lax.optimization_barrier(jnp.mean(values, axis=reduce_axis, keepdims=True))
    centred = values - centre
    spread = lax.optimization_barrier(jnp.mean(centred * centred, axis=reduce_axis, keepdims=True))
    return centred * lax.rsqrt(spread + epsilon)

def update_layer(pair, pair_mask, layer_index, incoming, in_gain, in_bias, projections, gate_weight, out_gain, out_bias, out_weight):
    pair_float = pair.astype(jnp.float32)
    normed = (normalize(pair_float, 2) * in_gain[layer_index] + in_bias[layer_index]).astype(jnp.bfloat16)
    projected = jnp.einsum('ikc,qch->qikh', normed.astype(jnp.float32), projections[layer_index].astype(jnp.float32), precision=lax.Precision.HIGHEST)
    left_edges = (jax.nn.sigmoid(projected[0]) * projected[1] * pair_mask).astype(jnp.bfloat16)
    right_edges = (jax.nn.sigmoid(projected[2]) * projected[3] * pair_mask).astype(jnp.bfloat16)
    if incoming:
        triangle = jnp.einsum('kih,kjh->ijh', left_edges.astype(jnp.float32), right_edges.astype(jnp.float32), precision=lax.Precision.HIGHEST)
    else:
        triangle = jnp.einsum('ikh,jkh->ijh', left_edges.astype(jnp.float32), right_edges.astype(jnp.float32), precision=lax.Precision.HIGHEST)
    triangle = triangle.astype(jnp.bfloat16)
    scaled = (normalize(triangle.astype(jnp.float32), 2) * out_gain[layer_index] + out_bias[layer_index]).astype(jnp.bfloat16)
    update = jnp.einsum('ijh,hc->ijc', scaled.astype(jnp.float32), out_weight[layer_index].astype(jnp.float32), precision=lax.Precision.HIGHEST)
    gating = jax.nn.sigmoid(jnp.einsum('ijc,cd->ijd', normed.astype(jnp.float32), gate_weight[layer_index].astype(jnp.float32), precision=lax.Precision.HIGHEST))
    return (pair_float + gating * update).astype(jnp.bfloat16)

def reference(pair, residue_mask, in_gain, in_bias, projections, gate_weight, out_gain, out_bias, out_weight):
    mask_float = residue_mask.astype(jnp.float32)
    pair_mask = mask_float[:, None, None] * mask_float[None, :, None]
    layer_one = update_layer(pair, pair_mask, 0, False, in_gain, in_bias, projections, gate_weight, out_gain, out_bias, out_weight)
    return update_layer(layer_one, pair_mask, 1, True, in_gain, in_bias, projections, gate_weight, out_gain, out_bias, out_weight)
```

```python
import functools

import jax
import jax.numpy as jnp
from jax import lax
from jax.experimental import pallas as pl
from jax.experimental.pallas import tpu as pltpu
from jax.sharding import PartitionSpec as P

epsilon = 1e-05
chunk_pixels = 256
MESH = pl.DeviceIdType.MESH


def normalize(values):
    centre = jnp.mean(values, axis=-1, keepdims=True)
    centred = values - centre
    spread = jnp.mean(centred * centred, axis=-1, keepdims=True)
    return centred * lax.rsqrt(spread + epsilon)


def sigmoid(values):
    return 0.5 * jnp.tanh(0.5 * values) + 0.5


def matmul(values, weight):
    flat = values.astype(jnp.bfloat16).reshape(-1, values.shape[-1])
    out = jnp.dot(flat, weight, preferred_element_type=jnp.float32)
    return out.reshape(values.shape[:-1] + (weight.shape[-1],))


def repeat(count, body):
    if count <= 8:
        for step in range(count):
            body(step)
    else:
        lax.fori_loop(0, count, lambda step, _: (body(step), 0)[1], 0)


def kernel(
    sizes,
    pair_ref,
    mask_ref,
    in_gain_ref,
    in_bias_ref,
    proj_ref,
    gate_ref,
    out_gain_ref,
    out_bias_ref,
    weight_ref,
    out_ref,
    left_rows,
    right_rows,
    pieces,
    tiles,
    mine,
    full,
    in_gain,
    in_bias,
    gate,
    out_gain,
    out_bias,
    weight,
    mask_cols,
    residual,
    normed,
    edges,
    triangle,
    edges_one,
    local_sem,
    first_send,
    left_recv,
    right_recv,
    piece_send,
    piece_recv,
    tile_send,
    tile_recv,
):
    zs, chan, sub, block, length = sizes
    chip_rows = sub * block
    width = length // (chan * sub)
    per_tile = width // block
    z, x, s = lax.axis_index("rows"), lax.axis_index("chan"), lax.axis_index("sub")
    own_block = z * sub + s
    tile = s * chan + x
    tile_part, tile_slot = tile // sub, tile % sub

    def device(dz, dx, ds):
        return {"rows": dz, "chan": dx, "sub": ds}

    small = [
        pltpu.make_async_copy(source, target, local_sem.at[index])
        for index, (source, target) in enumerate(
            (
                (pair_ref, left_rows.at[pl.ds(s * block, block)]),
                (proj_ref.at[0], pieces.at[x, 0]),
                (proj_ref.at[1], pieces.at[x, 1]),
                (in_gain_ref, in_gain),
                (in_bias_ref, in_bias),
                (gate_ref, gate),
                (out_gain_ref, out_gain),
                (out_bias_ref, out_bias),
                (weight_ref, weight),
            )
        )
    ]
    for copy in small:
        copy.start()

    barrier = pltpu.get_barrier_semaphore()
    others = chan * sub

    def greet(dz):
        for inner in range(others):
            dx, ds = inner // sub, inner % sub

            def signal():
                pl.semaphore_signal(
                    barrier,
                    inc=1,
                    device_id=device((z + dz) % zs, (x + dx) % chan, (s + ds) % sub),
                    device_id_type=MESH,
                )

            if inner == 0:
                if isinstance(dz, int):
                    if dz != 0:
                        signal()
                else:
                    pl.when(dz != 0)(signal)
            else:
                signal()

    repeat(zs, greet)
    pl.semaphore_wait(barrier, zs * others - 1)

    target_tile = own_block // per_tile
    target_x, target_s = target_tile % chan, target_tile // chan
    slot = own_block % per_tile

    def left_copy(ds):
        return pltpu.make_async_remote_copy(
            src_ref=pair_ref,
            dst_ref=left_rows.at[pl.ds(s * block, block)],
            send_sem=first_send.at[zs + ds - 1],
            recv_sem=left_recv.at[s],
            device_id=device(z, x, (s + ds) % sub),
            device_id_type=MESH,
        )

    def right_copy(dest_z):
        return pltpu.make_async_remote_copy(
            src_ref=pair_ref,
            dst_ref=right_rows.at[pl.ds(slot * block, block)],
            send_sem=first_send.at[dest_z],
            recv_sem=right_recv.at[slot],
            device_id=device(dest_z, x, target_s),
            device_id_type=MESH,
        )

    def sends_right(dest_z):
        return (x == target_x) & ((dest_z != z) | (target_s != s))

    def piece_copy(layer, dx):
        return pltpu.make_async_remote_copy(
            src_ref=proj_ref.at[layer],
            dst_ref=pieces.at[x, layer],
            send_sem=piece_send.at[layer, dx - 1],
            recv_sem=piece_recv.at[layer, x],
            device_id=device(z, (x + dx) % chan, s),
            device_id_type=MESH,
        )

    for dx in range(1, chan):
        piece_copy(0, dx).start()
    repeat(zs, lambda dz: pl.when(sends_right(dz))(lambda: right_copy(dz).start()))
    for ds in range(1, sub):
        left_copy(ds).start()
    for dx in range(1, chan):
        piece_copy(1, dx).start()

    rows_iota = lax.broadcasted_iota(jnp.int32, (length, length), 0)
    cols_iota = lax.broadcasted_iota(jnp.int32, (length, length), 1)
    mask_row = mask_ref[...].astype(jnp.float32)
    mask_col = jnp.sum(jnp.where(rows_iota == cols_iota, mask_row, 0.0), axis=1, keepdims=True)
    mask_cols[...] = jnp.broadcast_to(mask_col, mask_cols.shape)

    for copy in small:
        copy.wait()

    def assemble(layer):
        for other in range(1, chan):
            source = (x + other) % chan
            pltpu.make_async_remote_copy(
                src_ref=proj_ref.at[layer],
                dst_ref=pieces.at[source, layer],
                send_sem=piece_send.at[layer, other - 1],
                recv_sem=piece_recv.at[layer, source],
                device_id=device(z, source, s),
                device_id_type=MESH,
            ).wait_recv()
        for q in range(4):
            full[layer, q] = jnp.concatenate(
                [pieces[c, layer, q] for c in range(chan)], axis=-1
            )

    def scaled_input(values, layer):
        return normalize(values) * in_gain[layer : layer + 1] + in_bias[layer : layer + 1]

    def gated(values, layer, q):
        return sigmoid(matmul(values, full[layer, q])) * matmul(values, full[layer, q + 1])

    def finish(values, normed_part, residual_part, layer):
        whole = values.astype(jnp.bfloat16).astype(jnp.float32)
        scaled = normalize(whole) * out_gain[layer : layer + 1] + out_bias[layer : layer + 1]
        update = matmul(scaled, weight[layer])
        gating = sigmoid(matmul(normed_part, gate[layer]))
        return residual_part + gating * update

    for ds in range(1, sub):
        source = (s + ds) % sub
        pltpu.make_async_remote_copy(
            src_ref=pair_ref,
            dst_ref=left_rows.at[pl.ds(source * block, block)],
            send_sem=first_send.at[zs + ds - 1],
            recv_sem=left_recv.at[source],
            device_id=device(z, x, source),
            device_id_type=MESH,
        ).wait_recv()
    assemble(0)

    step_rows = max(1, min(chunk_pixels // length, chip_rows, width))

    def left_step(step):
        rows = pl.ds(step * step_rows, step_rows)
        values = left_rows[rows].astype(jnp.float32)
        ready = scaled_input(values, 0)
        residual[rows] = values
        normed[rows] = ready
        edges[rows] = gated(ready, 0, 0)

    repeat(chip_rows // step_rows, left_step)

    def right_arrival(p):
        source = tile * per_tile + p
        where = pl.ds(p * block, block)

        @pl.when(source == own_block)
        def _():
            right_rows[where] = left_rows[pl.ds(s * block, block)]

        @pl.when(source != own_block)
        def _():
            pltpu.make_async_remote_copy(
                src_ref=pair_ref,
                dst_ref=right_rows.at[where],
                send_sem=first_send.at[0],
                recv_sem=right_recv.at[p],
                device_id=device(source // sub, x, source % sub),
                device_id_type=MESH,
            ).wait_recv()

    repeat(per_tile, right_arrival)

    def right_step(step):
        rows = pl.ds(step * step_rows, step_rows)
        values = right_rows[rows].astype(jnp.float32)
        right = gated(scaled_input(values, 0), 0, 2) * mask_cols[...]

        def one(i):
            triangle[i, rows] = jnp.sum(right * edges[i], axis=1)

        repeat(chip_rows, one)

    repeat(width // step_rows, right_step)

    columns = pl.ds(pl.multiple_of(tile * width, width), width)
    mask_i = mask_cols[pl.ds(pl.multiple_of(z * chip_rows, chip_rows), chip_rows)]
    masked = triangle[...] * mask_cols[columns] * mask_i.reshape(chip_rows, 1, -1)
    layer_one = finish(masked, normed[:, columns], residual[:, columns], 0).astype(jnp.bfloat16)
    mine[...] = layer_one

    def tile_copy(place, dest, index):
        return pltpu.make_async_remote_copy(
            src_ref=mine,
            dst_ref=tiles.at[place, z],
            send_sem=tile_send.at[index],
            recv_sem=tile_recv.at[place, z],
            device_id=device(*dest),
            device_id_type=MESH,
        )

    def column_target(dz, ds):
        return ((z + dz) % zs, tile_part, (s + ds) % sub)

    def row_target(p, dx):
        target = tile * per_tile + p
        return (target // sub, (tile_part + dx) % chan, target % sub)

    def is_self(dest):
        return (dest[0] == z) & (dest[1] == x) & (dest[2] == s)

    def each_send(act):
        def over_rows(p):
            for dx in range(1, chan):
                dest = row_target(p, dx)
                index = zs * sub + p * (chan - 1) + dx - 1
                pl.when(jnp.logical_not(is_self(dest)))(
                    lambda: act(tile_copy(sub, dest, index))
                )

        def over_columns(dz):
            for ds in range(sub):
                dest = column_target(dz, ds)
                pl.when(jnp.logical_not(is_self(dest)))(
                    lambda: act(tile_copy(tile_slot, dest, dz * sub + ds))
                )

        repeat(zs, over_columns)
        repeat(per_tile, over_rows)

    each_send(lambda copy: copy.start())

    row_tile = own_block // per_tile
    row_part = row_tile // sub
    row_place = jnp.where(row_part == x, row_tile % sub, sub)

    @pl.when(tile_part == x)
    def _():
        tiles[tile_slot, z] = layer_one

    @pl.when((row_tile == tile) & (row_part != x))
    def _():
        tiles[sub, z] = layer_one

    assemble(1)

    def tile_wait(place, source_tile, source_z):
        source = (source_z, source_tile % chan, source_tile // chan)

        @pl.when(jnp.logical_not(is_self(source)))
        def _():
            pltpu.make_async_remote_copy(
                src_ref=mine,
                dst_ref=tiles.at[place, source_z],
                send_sem=tile_send.at[0],
                recv_sem=tile_recv.at[place, source_z],
                device_id=device(*source),
                device_id_type=MESH,
            ).wait_recv()

    for q in range(sub):
        repeat(zs, lambda source_z: tile_wait(q, x * sub + q, source_z))

    @pl.when(row_part != x)
    def _():
        repeat(zs, lambda source_z: tile_wait(sub, row_tile, source_z))

    step_z = max(1, min(chunk_pixels // (chip_rows * width), zs))

    def edge_step(step):
        planes = pl.ds(step * step_z, step_z)
        values = tiles[row_place, planes].astype(jnp.float32)
        edges_one[planes] = gated(scaled_input(values, 1), 1, 0)

    repeat(zs // step_z, edge_step)

    row_offset = (own_block % per_tile) * block
    results = []
    for q in range(sub):

        def tri_step(step, totals):
            planes = pl.ds(step * step_z, step_z)
            values = tiles[q, planes].astype(jnp.float32)
            right = gated(scaled_input(values, 1), 1, 2)
            k_start = step * step_z * chip_rows
            if not isinstance(step, int):
                k_start = pl.multiple_of(k_start, chip_rows)
            mask_k = mask_cols[pl.ds(k_start, step_z * chip_rows)]
            right = right * mask_k.reshape(step_z, chip_rows, 1, -1)
            return tuple(
                total
                + jnp.sum(
                    right * edges_one[planes, :, pl.ds(row_offset + i, 1)], axis=(0, 1)
                )
                for i, total in enumerate(totals)
            )

        totals = tuple(jnp.zeros((width, in_gain.shape[-1]), jnp.float32) for _ in range(block))
        if zs // step_z == 1:
            totals = tri_step(0, totals)
        else:
            totals = lax.fori_loop(0, zs // step_z, tri_step, totals)
        start = pl.multiple_of((x * sub + q) * width, width)
        mask_j = mask_cols[pl.ds(start, width)]
        mask_i = [mask_cols[pl.ds(own_block * block + i, 1)] for i in range(block)]
        masked = jnp.stack([total * mask_j * m for total, m in zip(totals, mask_i)])
        own = tiles[q, z, pl.ds(s * block, block)].astype(jnp.float32)
        results.append(finish(masked, scaled_input(own, 1), own, 1))
    out_ref[...] = jnp.concatenate(results, axis=1).astype(out_ref.dtype)

    for ds in range(1, sub):
        left_copy(ds).wait_send()
    repeat(zs, lambda dz: pl.when(sends_right(dz))(lambda: right_copy(dz).wait_send()))
    for layer in range(2):
        for dx in range(1, chan):
            piece_copy(layer, dx).wait_send()
    each_send(lambda copy: copy.wait_send())


def shards(sizes, pair, residue_mask, in_gain, in_bias, projections, gate_weight, out_gain, out_bias, out_weight):
    zs, chan, sub = sizes
    block, length, channels = pair.shape
    layers, kinds, _, part = projections.shape
    hidden = part * chan
    chip_rows = sub * block
    width = length // (chan * sub)
    per_tile = width // block
    f32, bf16 = jnp.float32, jnp.bfloat16
    dma = pltpu.SemaphoreType.DMA
    hbm = pl.BlockSpec(memory_space=pl.ANY)
    vmem = pl.BlockSpec(memory_space=pltpu.VMEM)
    return pl.pallas_call(
        functools.partial(kernel, (zs, chan, sub, block, length)),
        out_shape=jax.ShapeDtypeStruct((block, length // chan, channels), bf16),
        in_specs=[hbm, vmem] + [hbm] * 7,
        out_specs=vmem,
        scratch_shapes=[
            pltpu.VMEM((chip_rows, length, channels), bf16),
            pltpu.VMEM((width, length, channels), bf16),
            pltpu.VMEM((chan, layers, kinds, channels, part), bf16),
            pltpu.VMEM((sub + 1, zs, chip_rows, width, channels), bf16),
            pltpu.VMEM((chip_rows, width, channels), bf16),
            pltpu.VMEM((layers, kinds, channels, hidden), bf16),
            pltpu.VMEM(in_gain.shape, f32),
            pltpu.VMEM(in_bias.shape, f32),
            pltpu.VMEM(gate_weight.shape, bf16),
            pltpu.VMEM(out_gain.shape, f32),
            pltpu.VMEM(out_bias.shape, f32),
            pltpu.VMEM(out_weight.shape, bf16),
            pltpu.VMEM((length, hidden), f32),
            pltpu.VMEM((chip_rows, length, channels), f32),
            pltpu.VMEM((chip_rows, length, channels), f32),
            pltpu.VMEM((chip_rows, length, hidden), f32),
            pltpu.VMEM((chip_rows, width, hidden), f32),
            pltpu.VMEM((zs, chip_rows, width, hidden), f32),
            dma((9,)),
            dma((zs + sub,)),
            dma((sub,)),
            dma((per_tile,)),
            dma((layers, chan)),
            dma((layers, chan)),
            dma((zs * sub + per_tile * chan,)),
            dma((sub + 1, zs)),
        ],
        compiler_params=pltpu.CompilerParams(
            collective_id=0, has_side_effects=True, vmem_limit_bytes=56 * 2**20
        ),
    )(
        pair,
        residue_mask.reshape(1, length),
        in_gain,
        in_bias,
        projections,
        gate_weight,
        out_gain,
        out_bias,
        out_weight,
    )


def solution(mesh):
    sizes = (mesh.shape["rows"], mesh.shape["chan"], mesh.shape["sub"])
    placed = (
        P(("crops", "rows", "sub"), None, None),
        P("crops"),
        P(),
        P(),
        P(None, None, None, "chan"),
        P(),
        P(),
        P(),
        P(),
    )
    return jax.shard_map(
        functools.partial(shards, sizes),
        mesh=mesh,
        in_specs=placed,
        out_specs=P(("crops", "rows", "sub"), "chan", None),
        check_vma=False,
    )
```

```python
import functools

import jax
import jax.numpy as jnp
from jax import lax
from jax.experimental import pallas as pl
from jax.experimental.pallas import tpu as pltpu
from jax.sharding import PartitionSpec as P

epsilon = 1e-05
chunk_pixels = 256
MESH = pl.DeviceIdType.MESH


def normalize(values):
    centre = jnp.mean(values, axis=-1, keepdims=True)
    centred = values - centre
    spread = jnp.mean(centred * centred, axis=-1, keepdims=True)
    return centred * lax.rsqrt(spread + epsilon)


def sigmoid(values):
    return 0.5 * jnp.tanh(0.5 * values) + 0.5


def matmul(values, weight):
    flat = values.astype(jnp.bfloat16).reshape(-1, values.shape[-1])
    out = jnp.dot(flat, weight, preferred_element_type=jnp.float32)
    return out.reshape(values.shape[:-1] + (weight.shape[-1],))


def matmul_transposed(values, weight):
    flat = values.astype(jnp.bfloat16).reshape(-1, values.shape[-1])
    out = lax.dot_general(
        flat, weight, (((1,), (1,)), ((), ())), preferred_element_type=jnp.float32
    )
    return out.reshape(values.shape[:-1] + (weight.shape[0],))


def repeat(count, body):
    if count <= 8:
        for step in range(count):
            body(step)
    else:
        lax.fori_loop(0, count, lambda step, _: (body(step), 0)[1], 0)


def kernel(
    sizes,
    pair_ref,
    mask_ref,
    in_gain_ref,
    in_bias_ref,
    proj_ref,
    gate_ref,
    out_gain_ref,
    out_bias_ref,
    weight_ref,
    out_ref,
    left_rows,
    right_rows,
    tiles,
    mine,
    full,
    in_gain,
    in_bias,
    gate,
    out_gain,
    out_bias,
    weight,
    mask_cols,
    residual,
    normed,
    edges,
    triangle,
    edges_one,
    local_sem,
    first_send,
    left_recv,
    right_recv,
    piece_send,
    piece_recv,
    tile_send,
    tile_recv,
):
    zs, chan, sub, block, length = sizes
    chip_rows = sub * block
    width = length // (chan * sub)
    per_tile = width // block
    z, x, s = lax.axis_index("rows"), lax.axis_index("chan"), lax.axis_index("sub")
    own_block = z * sub + s
    tile = s * chan + x
    tile_part, tile_slot = tile // sub, tile % sub

    def device(dz, dx, ds):
        return {"rows": dz, "chan": dx, "sub": ds}

    part = proj_ref.shape[2]
    own_part = pl.ds(pl.multiple_of(x * part, part), part)

    small = [
        pltpu.make_async_copy(source, target, local_sem.at[index])
        for index, (source, target) in enumerate(
            (
                (pair_ref, left_rows.at[pl.ds(s * block, block)]),
                (proj_ref.at[0], full.at[0, :, own_part]),
                (proj_ref.at[1], full.at[1, :, own_part]),
                (in_gain_ref, in_gain),
                (in_bias_ref, in_bias),
                (gate_ref, gate),
                (out_gain_ref, out_gain),
                (out_bias_ref, out_bias),
                (weight_ref, weight),
            )
        )
    ]
    for copy in small:
        copy.start()

    barrier = pltpu.get_barrier_semaphore()
    others = chan * sub

    def greet(dz):
        for inner in range(others):
            dx, ds = inner // sub, inner % sub

            def signal():
                pl.semaphore_signal(
                    barrier,
                    inc=1,
                    device_id=device((z + dz) % zs, (x + dx) % chan, (s + ds) % sub),
                    device_id_type=MESH,
                )

            if inner == 0:
                if isinstance(dz, int):
                    if dz != 0:
                        signal()
                else:
                    pl.when(dz != 0)(signal)
            else:
                signal()

    repeat(zs, greet)
    pl.semaphore_wait(barrier, zs * others - 1)

    target_tile = own_block // per_tile
    target_x, target_s = target_tile % chan, target_tile // chan
    slot = own_block % per_tile

    def left_copy(ds):
        return pltpu.make_async_remote_copy(
            src_ref=pair_ref,
            dst_ref=left_rows.at[pl.ds(s * block, block)],
            send_sem=first_send.at[zs + ds - 1],
            recv_sem=left_recv.at[s],
            device_id=device(z, x, (s + ds) % sub),
            device_id_type=MESH,
        )

    def right_copy(dest_z):
        return pltpu.make_async_remote_copy(
            src_ref=pair_ref,
            dst_ref=right_rows.at[pl.ds(slot * block, block)],
            send_sem=first_send.at[dest_z],
            recv_sem=right_recv.at[slot],
            device_id=device(dest_z, x, target_s),
            device_id_type=MESH,
        )

    def sends_right(dest_z):
        return (x == target_x) & ((dest_z != z) | (target_s != s))

    def piece_copy(layer, dx):
        return pltpu.make_async_remote_copy(
            src_ref=proj_ref.at[layer],
            dst_ref=full.at[layer, :, own_part],
            send_sem=piece_send.at[layer, dx - 1],
            recv_sem=piece_recv.at[layer, x],
            device_id=device(z, (x + dx) % chan, s),
            device_id_type=MESH,
        )

    for dx in range(1, chan):
        piece_copy(0, dx).start()
    repeat(zs, lambda dz: pl.when(sends_right(dz))(lambda: right_copy(dz).start()))
    for ds in range(1, sub):
        left_copy(ds).start()
    for dx in range(1, chan):
        piece_copy(1, dx).start()

    rows_iota = lax.broadcasted_iota(jnp.int32, (length, length), 0)
    cols_iota = lax.broadcasted_iota(jnp.int32, (length, length), 1)
    mask_row = mask_ref[...].astype(jnp.float32)
    mask_col = jnp.sum(jnp.where(rows_iota == cols_iota, mask_row, 0.0), axis=1, keepdims=True)
    mask_cols[...] = jnp.broadcast_to(mask_col, mask_cols.shape)

    for copy in small:
        copy.wait()

    def assemble(layer):
        for other in range(1, chan):
            source = (x + other) % chan
            pltpu.make_async_remote_copy(
                src_ref=proj_ref.at[layer],
                dst_ref=full.at[layer, :, pl.ds(pl.multiple_of(source * part, part), part)],
                send_sem=piece_send.at[layer, other - 1],
                recv_sem=piece_recv.at[layer, source],
                device_id=device(z, source, s),
                device_id_type=MESH,
            ).wait_recv()

    def scaled_input(values, layer):
        return normalize(values) * in_gain[layer : layer + 1] + in_bias[layer : layer + 1]

    def gated(values, layer, q):
        gate_part = matmul_transposed(values, full[layer, q])
        return sigmoid(gate_part) * matmul_transposed(values, full[layer, q + 1])

    def finish(values, normed_part, residual_part, layer):
        whole = values.astype(jnp.bfloat16).astype(jnp.float32)
        scaled = normalize(whole) * out_gain[layer : layer + 1] + out_bias[layer : layer + 1]
        update = matmul(scaled, weight[layer])
        gating = sigmoid(matmul(normed_part, gate[layer]))
        return residual_part + gating * update

    for ds in range(1, sub):
        source = (s + ds) % sub
        pltpu.make_async_remote_copy(
            src_ref=pair_ref,
            dst_ref=left_rows.at[pl.ds(source * block, block)],
            send_sem=first_send.at[zs + ds - 1],
            recv_sem=left_recv.at[source],
            device_id=device(z, x, source),
            device_id_type=MESH,
        ).wait_recv()
    assemble(0)

    step_rows = max(1, min(chunk_pixels // length, chip_rows, width))

    def left_step(step):
        rows = pl.ds(step * step_rows, step_rows)
        values = left_rows[rows].astype(jnp.float32)
        ready = scaled_input(values, 0)
        residual[rows] = values
        normed[rows] = ready
        edges[rows] = gated(ready, 0, 0)

    repeat(chip_rows // step_rows, left_step)

    def right_arrival(p):
        source = tile * per_tile + p
        where = pl.ds(p * block, block)

        @pl.when(source == own_block)
        def _():
            right_rows[where] = left_rows[pl.ds(s * block, block)]

        @pl.when(source != own_block)
        def _():
            pltpu.make_async_remote_copy(
                src_ref=pair_ref,
                dst_ref=right_rows.at[where],
                send_sem=first_send.at[0],
                recv_sem=right_recv.at[p],
                device_id=device(source // sub, x, source % sub),
                device_id_type=MESH,
            ).wait_recv()

    repeat(per_tile, right_arrival)

    def right_step(step):
        rows = pl.ds(step * step_rows, step_rows)
        values = right_rows[rows].astype(jnp.float32)
        right = gated(scaled_input(values, 0), 0, 2) * mask_cols[...]

        def one(i):
            triangle[i, rows] = jnp.sum(right * edges[i], axis=1)

        repeat(chip_rows, one)

    repeat(width // step_rows, right_step)

    columns = pl.ds(pl.multiple_of(tile * width, width), width)
    mask_i = mask_cols[pl.ds(pl.multiple_of(z * chip_rows, chip_rows), chip_rows)]
    masked = triangle[...] * mask_cols[columns] * mask_i.reshape(chip_rows, 1, -1)
    layer_one = finish(masked, normed[:, columns], residual[:, columns], 0).astype(jnp.bfloat16)
    mine[...] = layer_one

    def tile_copy(place, dest, index):
        return pltpu.make_async_remote_copy(
            src_ref=mine,
            dst_ref=tiles.at[place, z],
            send_sem=tile_send.at[index],
            recv_sem=tile_recv.at[place, z],
            device_id=device(*dest),
            device_id_type=MESH,
        )

    def column_target(dz, ds):
        return ((z + dz) % zs, tile_part, (s + ds) % sub)

    def row_target(p, dx):
        target = tile * per_tile + p
        return (target // sub, (tile_part + dx) % chan, target % sub)

    def is_self(dest):
        return (dest[0] == z) & (dest[1] == x) & (dest[2] == s)

    def each_send(act):
        def over_rows(p):
            for dx in range(1, chan):
                dest = row_target(p, dx)
                index = zs * sub + p * (chan - 1) + dx - 1
                pl.when(jnp.logical_not(is_self(dest)))(
                    lambda: act(tile_copy(sub, dest, index))
                )

        def over_columns(dz):
            for ds in range(sub):
                dest = column_target(dz, ds)
                pl.when(jnp.logical_not(is_self(dest)))(
                    lambda: act(tile_copy(tile_slot, dest, dz * sub + ds))
                )

        repeat(zs, over_columns)
        repeat(per_tile, over_rows)

    each_send(lambda copy: copy.start())

    row_tile = own_block // per_tile
    row_part = row_tile // sub
    row_place = jnp.where(row_part == x, row_tile % sub, sub)

    @pl.when(tile_part == x)
    def _():
        tiles[tile_slot, z] = layer_one

    @pl.when((row_tile == tile) & (row_part != x))
    def _():
        tiles[sub, z] = layer_one

    assemble(1)

    def tile_wait(place, source_tile, source_z):
        source = (source_z, source_tile % chan, source_tile // chan)

        @pl.when(jnp.logical_not(is_self(source)))
        def _():
            pltpu.make_async_remote_copy(
                src_ref=mine,
                dst_ref=tiles.at[place, source_z],
                send_sem=tile_send.at[0],
                recv_sem=tile_recv.at[place, source_z],
                device_id=device(*source),
                device_id_type=MESH,
            ).wait_recv()

    for q in range(sub):
        repeat(zs, lambda source_z: tile_wait(q, x * sub + q, source_z))

    @pl.when(row_part != x)
    def _():
        repeat(zs, lambda source_z: tile_wait(sub, row_tile, source_z))

    step_z = max(1, min(chunk_pixels // (chip_rows * width), zs))

    def edge_step(step):
        planes = pl.ds(step * step_z, step_z)
        values = tiles[row_place, planes].astype(jnp.float32)
        edges_one[planes] = gated(scaled_input(values, 1), 1, 0)

    repeat(zs // step_z, edge_step)

    row_offset = (own_block % per_tile) * block
    results = []
    for q in range(sub):

        def tri_step(step, totals):
            planes = pl.ds(step * step_z, step_z)
            values = tiles[q, planes].astype(jnp.float32)
            right = gated(scaled_input(values, 1), 1, 2)
            k_start = step * step_z * chip_rows
            if not isinstance(step, int):
                k_start = pl.multiple_of(k_start, chip_rows)
            mask_k = mask_cols[pl.ds(k_start, step_z * chip_rows)]
            right = right * mask_k.reshape(step_z, chip_rows, 1, -1)
            return tuple(
                total
                + jnp.sum(
                    right * edges_one[planes, :, pl.ds(row_offset + i, 1)], axis=(0, 1)
                )
                for i, total in enumerate(totals)
            )

        totals = tuple(jnp.zeros((width, in_gain.shape[-1]), jnp.float32) for _ in range(block))
        if zs // step_z == 1:
            totals = tri_step(0, totals)
        else:
            totals = lax.fori_loop(0, zs // step_z, tri_step, totals)
        start = pl.multiple_of((x * sub + q) * width, width)
        mask_j = mask_cols[pl.ds(start, width)]
        mask_i = [mask_cols[pl.ds(own_block * block + i, 1)] for i in range(block)]
        masked = jnp.stack([total * mask_j * m for total, m in zip(totals, mask_i)])
        own = tiles[q, z, pl.ds(s * block, block)].astype(jnp.float32)
        results.append(finish(masked, scaled_input(own, 1), own, 1))
    out_ref[...] = jnp.concatenate(results, axis=1).astype(out_ref.dtype)

    for ds in range(1, sub):
        left_copy(ds).wait_send()
    repeat(zs, lambda dz: pl.when(sends_right(dz))(lambda: right_copy(dz).wait_send()))
    for layer in range(2):
        for dx in range(1, chan):
            piece_copy(layer, dx).wait_send()
    each_send(lambda copy: copy.wait_send())


def shards(sizes, pair, residue_mask, in_gain, in_bias, projections, gate_weight, out_gain, out_bias, out_weight):
    zs, chan, sub = sizes
    block, length, channels = pair.shape
    projections = jnp.swapaxes(projections, 2, 3)
    layers, kinds, part, _ = projections.shape
    hidden = part * chan
    chip_rows = sub * block
    width = length // (chan * sub)
    per_tile = width // block
    f32, bf16 = jnp.float32, jnp.bfloat16
    dma = pltpu.SemaphoreType.DMA
    hbm = pl.BlockSpec(memory_space=pl.ANY)
    vmem = pl.BlockSpec(memory_space=pltpu.VMEM)
    return pl.pallas_call(
        functools.partial(kernel, (zs, chan, sub, block, length)),
        out_shape=jax.ShapeDtypeStruct((block, length // chan, channels), bf16),
        in_specs=[hbm, vmem] + [hbm] * 7,
        out_specs=vmem,
        scratch_shapes=[
            pltpu.VMEM((chip_rows, length, channels), bf16),
            pltpu.VMEM((width, length, channels), bf16),
            pltpu.VMEM((sub + 1, zs, chip_rows, width, channels), bf16),
            pltpu.VMEM((chip_rows, width, channels), bf16),
            pltpu.VMEM((layers, kinds, hidden, channels), bf16),
            pltpu.VMEM(in_gain.shape, f32),
            pltpu.VMEM(in_bias.shape, f32),
            pltpu.VMEM(gate_weight.shape, bf16),
            pltpu.VMEM(out_gain.shape, f32),
            pltpu.VMEM(out_bias.shape, f32),
            pltpu.VMEM(out_weight.shape, bf16),
            pltpu.VMEM((length, hidden), f32),
            pltpu.VMEM((chip_rows, length, channels), f32),
            pltpu.VMEM((chip_rows, length, channels), f32),
            pltpu.VMEM((chip_rows, length, hidden), f32),
            pltpu.VMEM((chip_rows, width, hidden), f32),
            pltpu.VMEM((zs, chip_rows, width, hidden), f32),
            dma((9,)),
            dma((zs + sub,)),
            dma((sub,)),
            dma((per_tile,)),
            dma((layers, chan)),
            dma((layers, chan)),
            dma((zs * sub + per_tile * chan,)),
            dma((sub + 1, zs)),
        ],
        compiler_params=pltpu.CompilerParams(
            collective_id=0, has_side_effects=True, vmem_limit_bytes=56 * 2**20
        ),
    )(
        pair,
        residue_mask.reshape(1, length),
        in_gain,
        in_bias,
        projections,
        gate_weight,
        out_gain,
        out_bias,
        out_weight,
    )


def solution(mesh):
    sizes = (mesh.shape["rows"], mesh.shape["chan"], mesh.shape["sub"])
    placed = (
        P(("crops", "rows", "sub"), None, None),
        P("crops"),
        P(),
        P(),
        P(None, None, None, "chan"),
        P(),
        P(),
        P(),
        P(),
    )
    return jax.shard_map(
        functools.partial(shards, sizes),
        mesh=mesh,
        in_specs=placed,
        out_specs=P(("crops", "rows", "sub"), "chan", None),
        check_vma=False,
    )
```

```python
import functools

import jax
import jax.numpy as jnp
from jax import lax
from jax.experimental import pallas as pl
from jax.experimental.pallas import tpu as pltpu
from jax.sharding import PartitionSpec as P

epsilon = 1e-05
chunk_pixels = 256
MESH = pl.DeviceIdType.MESH


def normalize(values):
    centre = jnp.mean(values, axis=-1, keepdims=True)
    centred = values - centre
    spread = jnp.mean(centred * centred, axis=-1, keepdims=True)
    return centred * lax.rsqrt(spread + epsilon)


def sigmoid(values):
    return 0.5 * jnp.tanh(0.5 * values) + 0.5


def matmul(values, weight):
    flat = values.astype(jnp.bfloat16).reshape(-1, values.shape[-1])
    out = jnp.dot(flat, weight, preferred_element_type=jnp.float32)
    return out.reshape(values.shape[:-1] + (weight.shape[-1],))


def matmul_transposed(values, weight):
    flat = values.astype(jnp.bfloat16).reshape(-1, values.shape[-1])
    out = lax.dot_general(
        flat, weight, (((1,), (1,)), ((), ())), preferred_element_type=jnp.float32
    )
    return out.reshape(values.shape[:-1] + (weight.shape[0],))


def repeat(count, body):
    if count <= 8:
        for step in range(count):
            body(step)
    else:
        lax.fori_loop(0, count, lambda step, _: (body(step), 0)[1], 0)


def kernel(
    sizes,
    pair_ref,
    mask_ref,
    in_gain_ref,
    in_bias_ref,
    proj_ref,
    gate_ref,
    out_gain_ref,
    out_bias_ref,
    weight_ref,
    out_ref,
    left_rows,
    right_rows,
    tiles,
    full,
    in_gain,
    in_bias,
    gate,
    out_gain,
    out_bias,
    weight,
    mask_cols,
    residual,
    normed,
    edges,
    triangle,
    edges_one,
    local_sem,
    left_send,
    left_recv,
    right_send,
    right_recv,
    piece_send,
    piece_recv,
    tile_send,
    relay_send,
    row_send,
    tile_recv,
    wave,
):
    zs, chan, sub, block, length = sizes
    chip_rows = sub * block
    width = length // (chan * sub)
    per_tile = width // block
    z, x, s = lax.axis_index("rows"), lax.axis_index("chan"), lax.axis_index("sub")
    own_block = z * sub + s
    tile = x * sub + s
    last = zs - 1

    def device(dz, dx, ds):
        return {"rows": dz, "chan": dx, "sub": ds}

    part = proj_ref.shape[2]
    own_part = pl.ds(pl.multiple_of(x * part, part), part)

    small = [
        pltpu.make_async_copy(source, target, local_sem.at[index])
        for index, (source, target) in enumerate(
            (
                (pair_ref, left_rows.at[pl.ds(s * block, block)]),
                (proj_ref.at[0], full.at[0, :, own_part]),
                (proj_ref.at[1], full.at[1, :, own_part]),
                (in_gain_ref, in_gain),
                (in_bias_ref, in_bias),
                (gate_ref, gate),
                (out_gain_ref, out_gain),
                (out_bias_ref, out_bias),
                (weight_ref, weight),
            )
        )
    ]
    for copy in small:
        copy.start()

    barrier = pltpu.get_barrier_semaphore()

    def greet(*place):
        pl.semaphore_signal(
            barrier, inc=1, device_id=device(*place), device_id_type=MESH
        )

    for inner in range(1, chan * sub):
        greet(z, (x + inner // sub) % chan, (s + inner % sub) % sub)
    for ds in range(sub):
        pl.when(z > 0)(lambda: greet(z - 1, x, (s + ds) % sub))
        pl.when(z < last)(lambda: greet(z + 1, x, (s + ds) % sub))
    sides = jnp.where(z > 0, sub, 0) + jnp.where(z < last, sub, 0)
    pl.semaphore_wait(barrier, chan * sub - 1 + sides)

    target_tile = own_block // per_tile
    target_x, target_s = target_tile // sub, target_tile % sub
    slot = own_block % per_tile

    def left_copy(ds):
        return pltpu.make_async_remote_copy(
            src_ref=pair_ref,
            dst_ref=left_rows.at[pl.ds(s * block, block)],
            send_sem=left_send.at[ds],
            recv_sem=left_recv.at[s],
            device_id=device(z, x, (s + ds) % sub),
            device_id_type=MESH,
        )

    def right_copy(step):
        return pltpu.make_async_remote_copy(
            src_ref=pair_ref,
            dst_ref=right_rows.at[pl.ds(slot * block, block)],
            send_sem=right_send.at[per_tile + (step + 1) // 2],
            recv_sem=right_recv.at[slot],
            device_id=device(z + step, x, target_s),
            device_id_type=MESH,
        )

    def each_right(act):
        pl.when((x == target_x) & (z < last))(lambda: act(right_copy(1)))
        pl.when((x == target_x) & (z > 0))(lambda: act(right_copy(-1)))

    def forward_copy(p, step):
        where = pl.ds(p * block, block)
        return pltpu.make_async_remote_copy(
            src_ref=right_rows.at[where],
            dst_ref=right_rows.at[where],
            send_sem=right_send.at[p],
            recv_sem=right_recv.at[p],
            device_id=device(z + step, x, s),
            device_id_type=MESH,
        )

    def each_forward(p, act):
        source_z = (tile * per_tile + p) // sub
        pl.when((z > source_z) & (z < last))(lambda: act(forward_copy(p, 1)))
        pl.when((z < source_z) & (z > 0))(lambda: act(forward_copy(p, -1)))

    def piece_copy(layer, dx):
        return pltpu.make_async_remote_copy(
            src_ref=proj_ref.at[layer],
            dst_ref=full.at[layer, :, own_part],
            send_sem=piece_send.at[layer, dx - 1],
            recv_sem=piece_recv.at[layer, x],
            device_id=device(z, (x + dx) % chan, s),
            device_id_type=MESH,
        )

    each_right(lambda copy: copy.start())
    for ds in range(1, sub):
        left_copy(ds).start()
    for layer in range(2):
        for dx in range(1, chan):
            piece_copy(layer, dx).start()

    @pl.when((z == 0) & (z < last))
    def _():
        pl.semaphore_signal(
            wave.at[0], inc=1, device_id=device(z + 1, x, s), device_id_type=MESH
        )

    @pl.when((z == last) & (z > 0))
    def _():
        pl.semaphore_signal(
            wave.at[1], inc=1, device_id=device(z - 1, x, s), device_id_type=MESH
        )

    rows_iota = lax.broadcasted_iota(jnp.int32, (length, length), 0)
    cols_iota = lax.broadcasted_iota(jnp.int32, (length, length), 1)
    mask_row = mask_ref[...].astype(jnp.float32)
    mask_col = jnp.sum(jnp.where(rows_iota == cols_iota, mask_row, 0.0), axis=1, keepdims=True)
    mask_cols[...] = jnp.broadcast_to(mask_col, mask_cols.shape)

    for copy in small:
        copy.wait()

    def assemble(layer):
        for other in range(1, chan):
            source = (x + other) % chan
            pltpu.make_async_remote_copy(
                src_ref=proj_ref.at[layer],
                dst_ref=full.at[layer, :, pl.ds(pl.multiple_of(source * part, part), part)],
                send_sem=piece_send.at[layer, other - 1],
                recv_sem=piece_recv.at[layer, source],
                device_id=device(z, source, s),
                device_id_type=MESH,
            ).wait_recv()

    def scaled_input(values, layer):
        return normalize(values) * in_gain[layer : layer + 1] + in_bias[layer : layer + 1]

    def gated(values, layer, q):
        gate_part = matmul_transposed(values, full[layer, q])
        return sigmoid(gate_part) * matmul_transposed(values, full[layer, q + 1])

    def finish(values, normed_part, residual_part, layer):
        whole = values.astype(jnp.bfloat16).astype(jnp.float32)
        scaled = normalize(whole) * out_gain[layer : layer + 1] + out_bias[layer : layer + 1]
        update = matmul(scaled, weight[layer])
        gating = sigmoid(matmul(normed_part, gate[layer]))
        return residual_part + gating * update

    for ds in range(1, sub):
        source = (s + ds) % sub
        pltpu.make_async_remote_copy(
            src_ref=pair_ref,
            dst_ref=left_rows.at[pl.ds(source * block, block)],
            send_sem=left_send.at[ds],
            recv_sem=left_recv.at[source],
            device_id=device(z, x, source),
            device_id_type=MESH,
        ).wait_recv()

    def right_arrival(p):
        source = tile * per_tile + p
        where = pl.ds(p * block, block)

        @pl.when(source // sub == z)
        def _():
            right_rows[where] = left_rows[pl.ds((source % sub) * block, block)]

        @pl.when(source // sub != z)
        def _():
            forward_copy(p, 0).wait_recv()

        each_forward(p, lambda copy: copy.start())

    repeat(per_tile, right_arrival)

    @pl.when(z > 0)
    def _():
        pl.semaphore_wait(wave.at[0], 1)

        @pl.when(z < last)
        def _():
            pl.semaphore_signal(
                wave.at[0], inc=1, device_id=device(z + 1, x, s), device_id_type=MESH
            )

    @pl.when(z < last)
    def _():
        pl.semaphore_wait(wave.at[1], 1)

        @pl.when(z > 0)
        def _():
            pl.semaphore_signal(
                wave.at[1], inc=1, device_id=device(z - 1, x, s), device_id_type=MESH
            )

    assemble(0)

    step_rows = max(1, min(chunk_pixels // length, chip_rows, width))

    def left_step(step):
        rows = pl.ds(step * step_rows, step_rows)
        values = left_rows[rows].astype(jnp.float32)
        ready = scaled_input(values, 0)
        residual[rows] = values
        normed[rows] = ready
        edges[rows] = gated(ready, 0, 0)

    repeat(chip_rows // step_rows, left_step)

    def right_step(step):
        rows = pl.ds(step * step_rows, step_rows)
        values = right_rows[rows].astype(jnp.float32)
        right = gated(scaled_input(values, 0), 0, 2) * mask_cols[...]

        def one(i):
            triangle[i, rows] = jnp.sum(right * edges[i], axis=1)

        repeat(chip_rows, one)

    repeat(width // step_rows, right_step)

    columns = pl.ds(pl.multiple_of(tile * width, width), width)
    mask_i = mask_cols[pl.ds(pl.multiple_of(z * chip_rows, chip_rows), chip_rows)]
    masked = triangle[...] * mask_cols[columns] * mask_i.reshape(chip_rows, 1, -1)
    layer_one = finish(masked, normed[:, columns], residual[:, columns], 0).astype(jnp.bfloat16)
    tiles[s, z] = layer_one

    def tile_copy(place, source_z, send_sem, dest, source_place=s):
        return pltpu.make_async_remote_copy(
            src_ref=tiles.at[source_place, source_z],
            dst_ref=tiles.at[place, source_z],
            send_sem=send_sem,
            recv_sem=tile_recv.at[place, source_z],
            device_id=device(*dest),
            device_id_type=MESH,
        )

    def by_distance(act, distance):
        pl.when(z + distance < zs)(lambda: act(z + distance))
        pl.when(z - distance >= 0)(lambda: act(z - distance))

    def each_line(act):
        repeat(
            zs - 1,
            lambda step: by_distance(
                lambda dest_z: act(tile_copy(s, z, tile_send.at[dest_z], (dest_z, x, s))),
                zs - 1 - step,
            ),
        )

    def each_relay(source_z, act):
        for ds in range(1, sub):
            act(tile_copy(s, source_z, relay_send.at[ds, source_z], (z, x, (s + ds) % sub)))

    def each_row(act):
        def over_rows(p):
            target = tile * per_tile + p
            for dx in range(1, chan):
                dest = (target // sub, (x + dx) % chan, target % sub)
                act(tile_copy(sub, z, row_send.at[p, dx], dest))

        repeat(per_tile, over_rows)

    def start(copy):
        copy.start()

    each_line(start)
    each_relay(z, start)
    each_row(start)

    row_tile = own_block // per_tile
    row_part = row_tile // sub
    row_place = jnp.where(row_part == x, row_tile % sub, sub)
    assemble(1)

    def tile_wait(place, source_z):
        tile_copy(place, source_z, tile_send.at[0], (z, x, s)).wait_recv()

    def line_arrival(source_z):
        tile_wait(s, source_z)
        each_relay(source_z, start)

    repeat(zs - 1, lambda step: by_distance(line_arrival, step + 1))
    for ds in range(1, sub):
        repeat(zs, lambda source_z: tile_wait((s + ds) % sub, source_z))

    @pl.when(row_part != x)
    def _():
        repeat(zs, lambda source_z: tile_wait(sub, source_z))

    step_z = max(1, min(chunk_pixels // (chip_rows * width), zs))

    def edge_step(step):
        planes = pl.ds(step * step_z, step_z)
        values = tiles[row_place, planes].astype(jnp.float32)
        edges_one[planes] = gated(scaled_input(values, 1), 1, 0)

    repeat(zs // step_z, edge_step)

    row_offset = (own_block % per_tile) * block
    results = []
    for q in range(sub):

        def tri_step(step, totals):
            planes = pl.ds(step * step_z, step_z)
            values = tiles[q, planes].astype(jnp.float32)
            right = gated(scaled_input(values, 1), 1, 2)
            k_start = step * step_z * chip_rows
            if not isinstance(step, int):
                k_start = pl.multiple_of(k_start, chip_rows)
            mask_k = mask_cols[pl.ds(k_start, step_z * chip_rows)]
            right = right * mask_k.reshape(step_z, chip_rows, 1, -1)
            return tuple(
                total
                + jnp.sum(
                    right * edges_one[planes, :, pl.ds(row_offset + i, 1)], axis=(0, 1)
                )
                for i, total in enumerate(totals)
            )

        totals = tuple(jnp.zeros((width, in_gain.shape[-1]), jnp.float32) for _ in range(block))
        if zs // step_z == 1:
            totals = tri_step(0, totals)
        else:
            totals = lax.fori_loop(0, zs // step_z, tri_step, totals)
        start = pl.multiple_of((x * sub + q) * width, width)
        mask_j = mask_cols[pl.ds(start, width)]
        mask_i = [mask_cols[pl.ds(own_block * block + i, 1)] for i in range(block)]
        masked = jnp.stack([total * mask_j * m for total, m in zip(totals, mask_i)])
        own = tiles[q, z, pl.ds(s * block, block)].astype(jnp.float32)
        results.append(finish(masked, scaled_input(own, 1), own, 1))
    out_ref[...] = jnp.concatenate(results, axis=1).astype(out_ref.dtype)

    for ds in range(1, sub):
        left_copy(ds).wait_send()
    each_right(lambda copy: copy.wait_send())
    repeat(per_tile, lambda p: each_forward(p, lambda copy: copy.wait_send()))
    for layer in range(2):
        for dx in range(1, chan):
            piece_copy(layer, dx).wait_send()

    def wait_send(copy):
        copy.wait_send()

    each_line(wait_send)
    repeat(zs, lambda source_z: each_relay(source_z, wait_send))
    each_row(wait_send)


def shards(sizes, pair, residue_mask, in_gain, in_bias, projections, gate_weight, out_gain, out_bias, out_weight):
    zs, chan, sub = sizes
    block, length, channels = pair.shape
    projections = jnp.swapaxes(projections, 2, 3)
    layers, kinds, part, _ = projections.shape
    hidden = part * chan
    chip_rows = sub * block
    width = length // (chan * sub)
    per_tile = width // block
    f32, bf16 = jnp.float32, jnp.bfloat16
    dma = pltpu.SemaphoreType.DMA
    hbm = pl.BlockSpec(memory_space=pl.ANY)
    vmem = pl.BlockSpec(memory_space=pltpu.VMEM)
    return pl.pallas_call(
        functools.partial(kernel, (zs, chan, sub, block, length)),
        out_shape=jax.ShapeDtypeStruct((block, length // chan, channels), bf16),
        in_specs=[hbm, vmem] + [hbm] * 7,
        out_specs=vmem,
        scratch_shapes=[
            pltpu.VMEM((chip_rows, length, channels), bf16),
            pltpu.VMEM((width, length, channels), bf16),
            pltpu.VMEM((sub + 1, zs, chip_rows, width, channels), bf16),
            pltpu.VMEM((layers, kinds, hidden, channels), bf16),
            pltpu.VMEM(in_gain.shape, f32),
            pltpu.VMEM(in_bias.shape, f32),
            pltpu.VMEM(gate_weight.shape, bf16),
            pltpu.VMEM(out_gain.shape, f32),
            pltpu.VMEM(out_bias.shape, f32),
            pltpu.VMEM(out_weight.shape, bf16),
            pltpu.VMEM((length, hidden), f32),
            pltpu.VMEM((chip_rows, length, channels), f32),
            pltpu.VMEM((chip_rows, length, channels), f32),
            pltpu.VMEM((chip_rows, length, hidden), f32),
            pltpu.VMEM((chip_rows, width, hidden), f32),
            pltpu.VMEM((zs, chip_rows, width, hidden), f32),
            dma((9,)),
            dma((sub,)),
            dma((sub,)),
            dma((per_tile + 2,)),
            dma((per_tile,)),
            dma((layers, chan)),
            dma((layers, chan)),
            dma((zs,)),
            dma((sub, zs)),
            dma((per_tile, chan)),
            dma((sub + 1, zs)),
            pltpu.SemaphoreType.REGULAR((2,)),
        ],
        compiler_params=pltpu.CompilerParams(
            collective_id=0, has_side_effects=True, vmem_limit_bytes=56 * 2**20
        ),
    )(
        pair,
        residue_mask.reshape(1, length),
        in_gain,
        in_bias,
        projections,
        gate_weight,
        out_gain,
        out_bias,
        out_weight,
    )


def solution(mesh):
    sizes = (mesh.shape["rows"], mesh.shape["chan"], mesh.shape["sub"])
    placed = (
        P(("crops", "rows", "sub"), None, None),
        P("crops"),
        P(),
        P(),
        P(None, None, None, "chan"),
        P(),
        P(),
        P(),
        P(),
    )
    return jax.shard_map(
        functools.partial(shards, sizes),
        mesh=mesh,
        in_specs=placed,
        out_specs=P(("crops", "rows", "sub"), "chan", None),
        check_vma=False,
    )
```

```python
import functools

import jax
import jax.numpy as jnp
from jax import lax
from jax.experimental import pallas as pl
from jax.experimental.pallas import tpu as pltpu
from jax.sharding import PartitionSpec as P

epsilon = 1e-05
chunk_pixels = 256
MESH = pl.DeviceIdType.MESH


def normalize(values):
    centre = jnp.mean(values, axis=-1, keepdims=True)
    centred = values - centre
    spread = jnp.mean(centred * centred, axis=-1, keepdims=True)
    return centred * lax.rsqrt(spread + epsilon)


def sigmoid(values):
    return 0.5 * jnp.tanh(0.5 * values) + 0.5


def matmul(values, weight):
    flat = values.astype(jnp.bfloat16).reshape(-1, values.shape[-1])
    out = jnp.dot(flat, weight, preferred_element_type=jnp.float32)
    return out.reshape(values.shape[:-1] + (weight.shape[-1],))


def matmul_transposed(values, weight):
    flat = values.astype(jnp.bfloat16).reshape(-1, values.shape[-1])
    out = lax.dot_general(
        flat, weight, (((1,), (1,)), ((), ())), preferred_element_type=jnp.float32
    )
    return out.reshape(values.shape[:-1] + (weight.shape[0],))


def repeat(count, body):
    if count <= 8:
        for step in range(count):
            body(step)
    else:
        lax.fori_loop(0, count, lambda step, _: (body(step), 0)[1], 0)


def kernel(
    sizes,
    pair_ref,
    mask_ref,
    in_gain_ref,
    in_bias_ref,
    proj_ref,
    gate_ref,
    out_gain_ref,
    out_bias_ref,
    weight_ref,
    out_ref,
    left_rows,
    right_rows,
    tiles,
    mine,
    full,
    in_gain,
    in_bias,
    gate,
    out_gain,
    out_bias,
    weight,
    mask_cols,
    residual,
    normed,
    edges,
    triangle,
    edges_one,
    local_sem,
    first_send,
    left_recv,
    right_recv,
    piece_send,
    piece_recv,
    tile_send,
    tile_recv,
):
    zs, chan, sub, block, length = sizes
    chip_rows = sub * block
    width = length // (chan * sub)
    per_tile = width // block
    z, x, s = lax.axis_index("rows"), lax.axis_index("chan"), lax.axis_index("sub")
    own_block = z * sub + s
    tile = s * chan + x
    tile_part, tile_slot = tile // sub, tile % sub

    def device(dz, dx, ds):
        return {"rows": dz, "chan": dx, "sub": ds}

    part = proj_ref.shape[2]
    own_part = pl.ds(pl.multiple_of(x * part, part), part)

    def farthest_first(act):
        def at_distance(step):
            distance = zs - 1 - step
            pl.when(z + distance < zs)(lambda: act(z + distance))
            pl.when(z - distance >= 0)(lambda: act(z - distance))

        repeat(zs - 1, at_distance)
        act(z)

    small = [
        pltpu.make_async_copy(source, target, local_sem.at[index])
        for index, (source, target) in enumerate(
            (
                (pair_ref, left_rows.at[pl.ds(s * block, block)]),
                (proj_ref.at[0], full.at[0, :, own_part]),
                (proj_ref.at[1], full.at[1, :, own_part]),
                (in_gain_ref, in_gain),
                (in_bias_ref, in_bias),
                (gate_ref, gate),
                (out_gain_ref, out_gain),
                (out_bias_ref, out_bias),
                (weight_ref, weight),
            )
        )
    ]
    for copy in small:
        copy.start()

    barrier = pltpu.get_barrier_semaphore()
    others = chan * sub

    def greet(dz):
        for inner in range(others):
            dx, ds = inner // sub, inner % sub

            def signal():
                pl.semaphore_signal(
                    barrier,
                    inc=1,
                    device_id=device((z + dz) % zs, (x + dx) % chan, (s + ds) % sub),
                    device_id_type=MESH,
                )

            if inner == 0:
                if isinstance(dz, int):
                    if dz != 0:
                        signal()
                else:
                    pl.when(dz != 0)(signal)
            else:
                signal()

    repeat(zs, greet)
    pl.semaphore_wait(barrier, zs * others - 1)

    target_tile = own_block // per_tile
    target_x, target_s = target_tile % chan, target_tile // chan
    slot = own_block % per_tile

    def left_copy(ds):
        return pltpu.make_async_remote_copy(
            src_ref=pair_ref,
            dst_ref=left_rows.at[pl.ds(s * block, block)],
            send_sem=first_send.at[zs + ds - 1],
            recv_sem=left_recv.at[s],
            device_id=device(z, x, (s + ds) % sub),
            device_id_type=MESH,
        )

    def right_copy(dest_z):
        return pltpu.make_async_remote_copy(
            src_ref=pair_ref,
            dst_ref=right_rows.at[pl.ds(slot * block, block)],
            send_sem=first_send.at[dest_z],
            recv_sem=right_recv.at[slot],
            device_id=device(dest_z, x, target_s),
            device_id_type=MESH,
        )

    def sends_right(dest_z):
        return (x == target_x) & ((dest_z != z) | (target_s != s))

    def piece_copy(layer, dx):
        return pltpu.make_async_remote_copy(
            src_ref=proj_ref.at[layer],
            dst_ref=full.at[layer, :, own_part],
            send_sem=piece_send.at[layer, dx - 1],
            recv_sem=piece_recv.at[layer, x],
            device_id=device(z, (x + dx) % chan, s),
            device_id_type=MESH,
        )

    for dx in range(1, chan):
        piece_copy(0, dx).start()

    def start_right(dest_z):
        pl.when(sends_right(dest_z))(lambda: right_copy(dest_z).start())

    farthest_first(start_right)
    for ds in range(1, sub):
        left_copy(ds).start()
    for dx in range(1, chan):
        piece_copy(1, dx).start()

    rows_iota = lax.broadcasted_iota(jnp.int32, (length, length), 0)
    cols_iota = lax.broadcasted_iota(jnp.int32, (length, length), 1)
    mask_row = mask_ref[...].astype(jnp.float32)
    mask_col = jnp.sum(jnp.where(rows_iota == cols_iota, mask_row, 0.0), axis=1, keepdims=True)
    mask_cols[...] = jnp.broadcast_to(mask_col, mask_cols.shape)

    for copy in small:
        copy.wait()

    def assemble(layer):
        for other in range(1, chan):
            source = (x + other) % chan
            pltpu.make_async_remote_copy(
                src_ref=proj_ref.at[layer],
                dst_ref=full.at[layer, :, pl.ds(pl.multiple_of(source * part, part), part)],
                send_sem=piece_send.at[layer, other - 1],
                recv_sem=piece_recv.at[layer, source],
                device_id=device(z, source, s),
                device_id_type=MESH,
            ).wait_recv()

    def scaled_input(values, layer):
        return normalize(values) * in_gain[layer : layer + 1] + in_bias[layer : layer + 1]

    def gated(values, layer, q):
        gate_part = matmul_transposed(values, full[layer, q])
        return sigmoid(gate_part) * matmul_transposed(values, full[layer, q + 1])

    def finish(values, normed_part, residual_part, layer):
        whole = values.astype(jnp.bfloat16).astype(jnp.float32)
        scaled = normalize(whole) * out_gain[layer : layer + 1] + out_bias[layer : layer + 1]
        update = matmul(scaled, weight[layer])
        gating = sigmoid(matmul(normed_part, gate[layer]))
        return residual_part + gating * update

    for ds in range(1, sub):
        source = (s + ds) % sub
        pltpu.make_async_remote_copy(
            src_ref=pair_ref,
            dst_ref=left_rows.at[pl.ds(source * block, block)],
            send_sem=first_send.at[zs + ds - 1],
            recv_sem=left_recv.at[source],
            device_id=device(z, x, source),
            device_id_type=MESH,
        ).wait_recv()
    assemble(0)

    step_rows = max(1, min(chunk_pixels // length, chip_rows, width))

    def left_step(step):
        rows = pl.ds(step * step_rows, step_rows)
        values = left_rows[rows].astype(jnp.float32)
        ready = scaled_input(values, 0)
        residual[rows] = values
        normed[rows] = ready
        edges[rows] = gated(ready, 0, 0)

    repeat(chip_rows // step_rows, left_step)

    def right_arrival(p):
        source = tile * per_tile + p
        where = pl.ds(p * block, block)

        @pl.when(source == own_block)
        def _():
            right_rows[where] = left_rows[pl.ds(s * block, block)]

        @pl.when(source != own_block)
        def _():
            pltpu.make_async_remote_copy(
                src_ref=pair_ref,
                dst_ref=right_rows.at[where],
                send_sem=first_send.at[0],
                recv_sem=right_recv.at[p],
                device_id=device(source // sub, x, source % sub),
                device_id_type=MESH,
            ).wait_recv()

    repeat(per_tile, right_arrival)

    def right_step(step):
        rows = pl.ds(step * step_rows, step_rows)
        values = right_rows[rows].astype(jnp.float32)
        right = gated(scaled_input(values, 0), 0, 2) * mask_cols[...]

        def one(i):
            triangle[i, rows] = jnp.sum(right * edges[i], axis=1)

        repeat(chip_rows, one)

    repeat(width // step_rows, right_step)

    columns = pl.ds(pl.multiple_of(tile * width, width), width)
    mask_i = mask_cols[pl.ds(pl.multiple_of(z * chip_rows, chip_rows), chip_rows)]
    masked = triangle[...] * mask_cols[columns] * mask_i.reshape(chip_rows, 1, -1)
    layer_one = finish(masked, normed[:, columns], residual[:, columns], 0).astype(jnp.bfloat16)
    mine[...] = layer_one

    def tile_copy(place, dest, index):
        return pltpu.make_async_remote_copy(
            src_ref=mine,
            dst_ref=tiles.at[place, z],
            send_sem=tile_send.at[index],
            recv_sem=tile_recv.at[place, z],
            device_id=device(*dest),
            device_id_type=MESH,
        )

    def column_target(dest_z, ds):
        return (dest_z, tile_part, (s + ds) % sub)

    def row_target(p, dx):
        target = tile * per_tile + p
        return (target // sub, (tile_part + dx) % chan, target % sub)

    def is_self(dest):
        return (dest[0] == z) & (dest[1] == x) & (dest[2] == s)

    def each_send(act):
        def over_rows(p):
            for dx in range(1, chan):
                dest = row_target(p, dx)
                index = zs * sub + p * (chan - 1) + dx - 1
                pl.when(jnp.logical_not(is_self(dest)))(
                    lambda: act(tile_copy(sub, dest, index))
                )

        def over_columns(dest_z):
            for ds in range(sub):
                dest = column_target(dest_z, ds)
                pl.when(jnp.logical_not(is_self(dest)))(
                    lambda: act(tile_copy(tile_slot, dest, dest_z * sub + ds))
                )

        farthest_first(over_columns)
        repeat(per_tile, over_rows)

    each_send(lambda copy: copy.start())

    row_tile = own_block // per_tile
    row_part = row_tile // sub
    row_place = jnp.where(row_part == x, row_tile % sub, sub)

    @pl.when(tile_part == x)
    def _():
        tiles[tile_slot, z] = layer_one

    @pl.when((row_tile == tile) & (row_part != x))
    def _():
        tiles[sub, z] = layer_one

    assemble(1)

    def tile_wait(place, source_tile, source_z):
        source = (source_z, source_tile % chan, source_tile // chan)

        @pl.when(jnp.logical_not(is_self(source)))
        def _():
            pltpu.make_async_remote_copy(
                src_ref=mine,
                dst_ref=tiles.at[place, source_z],
                send_sem=tile_send.at[0],
                recv_sem=tile_recv.at[place, source_z],
                device_id=device(*source),
                device_id_type=MESH,
            ).wait_recv()

    for q in range(sub):
        repeat(zs, lambda source_z: tile_wait(q, x * sub + q, source_z))

    @pl.when(row_part != x)
    def _():
        repeat(zs, lambda source_z: tile_wait(sub, row_tile, source_z))

    step_z = max(1, min(chunk_pixels // (chip_rows * width), zs))

    def edge_step(step):
        planes = pl.ds(step * step_z, step_z)
        values = tiles[row_place, planes].astype(jnp.float32)
        edges_one[planes] = gated(scaled_input(values, 1), 1, 0)

    repeat(zs // step_z, edge_step)

    row_offset = (own_block % per_tile) * block
    results = []
    for q in range(sub):

        def tri_step(step, totals):
            planes = pl.ds(step * step_z, step_z)
            values = tiles[q, planes].astype(jnp.float32)
            right = gated(scaled_input(values, 1), 1, 2)
            k_start = step * step_z * chip_rows
            if not isinstance(step, int):
                k_start = pl.multiple_of(k_start, chip_rows)
            mask_k = mask_cols[pl.ds(k_start, step_z * chip_rows)]
            right = right * mask_k.reshape(step_z, chip_rows, 1, -1)
            return tuple(
                total
                + jnp.sum(
                    right * edges_one[planes, :, pl.ds(row_offset + i, 1)], axis=(0, 1)
                )
                for i, total in enumerate(totals)
            )

        totals = tuple(jnp.zeros((width, in_gain.shape[-1]), jnp.float32) for _ in range(block))
        if zs // step_z == 1:
            totals = tri_step(0, totals)
        else:
            totals = lax.fori_loop(0, zs // step_z, tri_step, totals)
        start = pl.multiple_of((x * sub + q) * width, width)
        mask_j = mask_cols[pl.ds(start, width)]
        mask_i = [mask_cols[pl.ds(own_block * block + i, 1)] for i in range(block)]
        masked = jnp.stack([total * mask_j * m for total, m in zip(totals, mask_i)])
        own = tiles[q, z, pl.ds(s * block, block)].astype(jnp.float32)
        results.append(finish(masked, scaled_input(own, 1), own, 1))
    out_ref[...] = jnp.concatenate(results, axis=1).astype(out_ref.dtype)

    for ds in range(1, sub):
        left_copy(ds).wait_send()
    repeat(zs, lambda dz: pl.when(sends_right(dz))(lambda: right_copy(dz).wait_send()))
    for layer in range(2):
        for dx in range(1, chan):
            piece_copy(layer, dx).wait_send()
    each_send(lambda copy: copy.wait_send())


def shards(sizes, pair, residue_mask, in_gain, in_bias, projections, gate_weight, out_gain, out_bias, out_weight):
    zs, chan, sub = sizes
    block, length, channels = pair.shape
    projections = jnp.swapaxes(projections, 2, 3)
    layers, kinds, part, _ = projections.shape
    hidden = part * chan
    chip_rows = sub * block
    width = length // (chan * sub)
    per_tile = width // block
    f32, bf16 = jnp.float32, jnp.bfloat16
    dma = pltpu.SemaphoreType.DMA
    hbm = pl.BlockSpec(memory_space=pl.ANY)
    vmem = pl.BlockSpec(memory_space=pltpu.VMEM)
    return pl.pallas_call(
        functools.partial(kernel, (zs, chan, sub, block, length)),
        out_shape=jax.ShapeDtypeStruct((block, length // chan, channels), bf16),
        in_specs=[hbm, vmem] + [hbm] * 7,
        out_specs=vmem,
        scratch_shapes=[
            pltpu.VMEM((chip_rows, length, channels), bf16),
            pltpu.VMEM((width, length, channels), bf16),
            pltpu.VMEM((sub + 1, zs, chip_rows, width, channels), bf16),
            pltpu.VMEM((chip_rows, width, channels), bf16),
            pltpu.VMEM((layers, kinds, hidden, channels), bf16),
            pltpu.VMEM(in_gain.shape, f32),
            pltpu.VMEM(in_bias.shape, f32),
            pltpu.VMEM(gate_weight.shape, bf16),
            pltpu.VMEM(out_gain.shape, f32),
            pltpu.VMEM(out_bias.shape, f32),
            pltpu.VMEM(out_weight.shape, bf16),
            pltpu.VMEM((length, hidden), f32),
            pltpu.VMEM((chip_rows, length, channels), f32),
            pltpu.VMEM((chip_rows, length, channels), f32),
            pltpu.VMEM((chip_rows, length, hidden), f32),
            pltpu.VMEM((chip_rows, width, hidden), f32),
            pltpu.VMEM((zs, chip_rows, width, hidden), f32),
            dma((9,)),
            dma((zs + sub,)),
            dma((sub,)),
            dma((per_tile,)),
            dma((layers, chan)),
            dma((layers, chan)),
            dma((zs * sub + per_tile * chan,)),
            dma((sub + 1, zs)),
        ],
        compiler_params=pltpu.CompilerParams(
            collective_id=0, has_side_effects=True, vmem_limit_bytes=56 * 2**20
        ),
    )(
        pair,
        residue_mask.reshape(1, length),
        in_gain,
        in_bias,
        projections,
        gate_weight,
        out_gain,
        out_bias,
        out_weight,
    )


def solution(mesh):
    sizes = (mesh.shape["rows"], mesh.shape["chan"], mesh.shape["sub"])
    placed = (
        P(("crops", "rows", "sub"), None, None),
        P("crops"),
        P(),
        P(),
        P(None, None, None, "chan"),
        P(),
        P(),
        P(),
        P(),
    )
    return jax.shard_map(
        functools.partial(shards, sizes),
        mesh=mesh,
        in_specs=placed,
        out_specs=P(("crops", "rows", "sub"), "chan", None),
        check_vma=False,
    )
```

```python
import functools

import jax
import jax.numpy as jnp
from jax import lax
from jax.experimental import pallas as pl
from jax.experimental.pallas import tpu as pltpu
from jax.sharding import PartitionSpec as P

epsilon = 1e-05
chunk_pixels = 256
MESH = pl.DeviceIdType.MESH


def normalize(values):
    centre = jnp.mean(values, axis=-1, keepdims=True)
    centred = values - centre
    spread = jnp.mean(centred * centred, axis=-1, keepdims=True)
    return centred * lax.rsqrt(spread + epsilon)


def sigmoid(values):
    return 0.5 * jnp.tanh(0.5 * values) + 0.5


def matmul(values, weight):
    flat = values.astype(jnp.bfloat16).reshape(-1, values.shape[-1])
    out = jnp.dot(flat, weight, preferred_element_type=jnp.float32)
    return out.reshape(values.shape[:-1] + (weight.shape[-1],))


def matmul_transposed(values, weight):
    flat = values.astype(jnp.bfloat16).reshape(-1, values.shape[-1])
    out = lax.dot_general(
        flat, weight, (((1,), (1,)), ((), ())), preferred_element_type=jnp.float32
    )
    return out.reshape(values.shape[:-1] + (weight.shape[0],))


def repeat(count, body):
    if count <= 8:
        for step in range(count):
            body(step)
    else:
        lax.fori_loop(0, count, lambda step, _: (body(step), 0)[1], 0)


def kernel(
    sizes,
    pair_ref,
    mask_ref,
    in_gain_ref,
    in_bias_ref,
    proj_ref,
    gate_ref,
    out_gain_ref,
    out_bias_ref,
    weight_ref,
    out_ref,
    left_rows,
    right_rows,
    tiles,
    mine,
    full,
    in_gain,
    in_bias,
    gate,
    out_gain,
    out_bias,
    weight,
    mask_cols,
    residual,
    normed,
    edges,
    triangle,
    edges_one,
    local_sem,
    first_send,
    left_recv,
    right_recv,
    piece_send,
    piece_recv,
    tile_send,
    tile_recv,
):
    zs, chan, sub, block, length = sizes
    chip_rows = sub * block
    width = length // (chan * sub)
    per_tile = width // block
    z, x, s = lax.axis_index("rows"), lax.axis_index("chan"), lax.axis_index("sub")
    own_block = z * sub + s
    tile = s * chan + x
    tile_part, tile_slot = tile // sub, tile % sub

    def device(dz, dx, ds):
        return {"rows": dz, "chan": dx, "sub": ds}

    part = proj_ref.shape[2]
    own_part = pl.ds(pl.multiple_of(x * part, part), part)
    own_rows = left_rows.at[pl.ds(s * block, block)]

    def farthest_first(act):
        def at_distance(step):
            distance = zs - 1 - step
            pl.when(z + distance < zs)(lambda: act(z + distance))
            pl.when(z - distance >= 0)(lambda: act(z - distance))

        repeat(zs - 1, at_distance)
        act(z)

    small = [
        pltpu.make_async_copy(source, target, local_sem.at[index])
        for index, (source, target) in enumerate(
            (
                (pair_ref, own_rows),
                (proj_ref.at[0], full.at[0, :, own_part]),
                (proj_ref.at[1], full.at[1, :, own_part]),
                (in_gain_ref, in_gain),
                (in_bias_ref, in_bias),
                (gate_ref, gate),
                (out_gain_ref, out_gain),
                (out_bias_ref, out_bias),
                (weight_ref, weight),
            )
        )
    ]
    for copy in small:
        copy.start()

    barrier = pltpu.get_barrier_semaphore()
    others = chan * sub

    def greet(dz):
        for inner in range(others):
            dx, ds = inner // sub, inner % sub

            def signal():
                pl.semaphore_signal(
                    barrier,
                    inc=1,
                    device_id=device((z + dz) % zs, (x + dx) % chan, (s + ds) % sub),
                    device_id_type=MESH,
                )

            if inner == 0:
                if isinstance(dz, int):
                    if dz != 0:
                        signal()
                else:
                    pl.when(dz != 0)(signal)
            else:
                signal()

    repeat(zs, greet)
    pl.semaphore_wait(barrier, zs * others - 1)

    for copy in small:
        copy.wait()

    target_tile = own_block // per_tile
    target_x, target_s = target_tile % chan, target_tile // chan
    slot = own_block % per_tile

    def left_copy(ds):
        return pltpu.make_async_remote_copy(
            src_ref=own_rows,
            dst_ref=left_rows.at[pl.ds(s * block, block)],
            send_sem=first_send.at[zs + ds - 1],
            recv_sem=left_recv.at[s],
            device_id=device(z, x, (s + ds) % sub),
            device_id_type=MESH,
        )

    def right_copy(dest_z):
        return pltpu.make_async_remote_copy(
            src_ref=own_rows,
            dst_ref=right_rows.at[pl.ds(slot * block, block)],
            send_sem=first_send.at[dest_z],
            recv_sem=right_recv.at[slot],
            device_id=device(dest_z, x, target_s),
            device_id_type=MESH,
        )

    def sends_right(dest_z):
        return (x == target_x) & ((dest_z != z) | (target_s != s))

    def piece_copy(layer, dx):
        return pltpu.make_async_remote_copy(
            src_ref=full.at[layer, :, own_part],
            dst_ref=full.at[layer, :, own_part],
            send_sem=piece_send.at[layer, dx - 1],
            recv_sem=piece_recv.at[layer, x],
            device_id=device(z, (x + dx) % chan, s),
            device_id_type=MESH,
        )

    for dx in range(1, chan):
        piece_copy(0, dx).start()

    def start_right(dest_z):
        pl.when(sends_right(dest_z))(lambda: right_copy(dest_z).start())

    farthest_first(start_right)
    for ds in range(1, sub):
        left_copy(ds).start()
    for dx in range(1, chan):
        piece_copy(1, dx).start()

    rows_iota = lax.broadcasted_iota(jnp.int32, (length, length), 0)
    cols_iota = lax.broadcasted_iota(jnp.int32, (length, length), 1)
    mask_row = mask_ref[...].astype(jnp.float32)
    mask_col = jnp.sum(jnp.where(rows_iota == cols_iota, mask_row, 0.0), axis=1, keepdims=True)
    mask_cols[...] = jnp.broadcast_to(mask_col, mask_cols.shape)

    def assemble(layer):
        for other in range(1, chan):
            source = (x + other) % chan
            pltpu.make_async_remote_copy(
                src_ref=full.at[layer, :, own_part],
                dst_ref=full.at[layer, :, pl.ds(pl.multiple_of(source * part, part), part)],
                send_sem=piece_send.at[layer, other - 1],
                recv_sem=piece_recv.at[layer, source],
                device_id=device(z, source, s),
                device_id_type=MESH,
            ).wait_recv()

    def scaled_input(values, layer):
        return normalize(values) * in_gain[layer : layer + 1] + in_bias[layer : layer + 1]

    def gated(values, layer, q):
        gate_part = matmul_transposed(values, full[layer, q])
        return sigmoid(gate_part) * matmul_transposed(values, full[layer, q + 1])

    def finish(values, normed_part, residual_part, layer):
        whole = values.astype(jnp.bfloat16).astype(jnp.float32)
        scaled = normalize(whole) * out_gain[layer : layer + 1] + out_bias[layer : layer + 1]
        update = matmul(scaled, weight[layer])
        gating = sigmoid(matmul(normed_part, gate[layer]))
        return residual_part + gating * update

    for ds in range(1, sub):
        source = (s + ds) % sub
        pltpu.make_async_remote_copy(
            src_ref=own_rows,
            dst_ref=left_rows.at[pl.ds(source * block, block)],
            send_sem=first_send.at[zs + ds - 1],
            recv_sem=left_recv.at[source],
            device_id=device(z, x, source),
            device_id_type=MESH,
        ).wait_recv()
    assemble(0)

    step_rows = max(1, min(chunk_pixels // length, chip_rows, width))

    def left_step(step):
        rows = pl.ds(step * step_rows, step_rows)
        values = left_rows[rows].astype(jnp.float32)
        ready = scaled_input(values, 0)
        residual[rows] = values
        normed[rows] = ready
        edges[rows] = gated(ready, 0, 0)

    repeat(chip_rows // step_rows, left_step)

    def right_arrival(p):
        source = tile * per_tile + p
        where = pl.ds(p * block, block)

        @pl.when(source == own_block)
        def _():
            right_rows[where] = left_rows[pl.ds(s * block, block)]

        @pl.when(source != own_block)
        def _():
            pltpu.make_async_remote_copy(
                src_ref=own_rows,
                dst_ref=right_rows.at[where],
                send_sem=first_send.at[0],
                recv_sem=right_recv.at[p],
                device_id=device(source // sub, x, source % sub),
                device_id_type=MESH,
            ).wait_recv()

    repeat(per_tile, right_arrival)

    def right_step(step):
        rows = pl.ds(step * step_rows, step_rows)
        values = right_rows[rows].astype(jnp.float32)
        right = gated(scaled_input(values, 0), 0, 2) * mask_cols[...]

        def one(i):
            triangle[i, rows] = jnp.sum(right * edges[i], axis=1)

        repeat(chip_rows, one)

    repeat(width // step_rows, right_step)

    columns = pl.ds(pl.multiple_of(tile * width, width), width)
    mask_i = mask_cols[pl.ds(pl.multiple_of(z * chip_rows, chip_rows), chip_rows)]
    masked = triangle[...] * mask_cols[columns] * mask_i.reshape(chip_rows, 1, -1)
    layer_one = finish(masked, normed[:, columns], residual[:, columns], 0).astype(jnp.bfloat16)
    mine[...] = layer_one

    def tile_copy(place, dest, index):
        return pltpu.make_async_remote_copy(
            src_ref=mine,
            dst_ref=tiles.at[place, z],
            send_sem=tile_send.at[index],
            recv_sem=tile_recv.at[place, z],
            device_id=device(*dest),
            device_id_type=MESH,
        )

    def column_target(dest_z, ds):
        return (dest_z, tile_part, (s + ds) % sub)

    def row_target(p, dx):
        target = tile * per_tile + p
        return (target // sub, (tile_part + dx) % chan, target % sub)

    def is_self(dest):
        return (dest[0] == z) & (dest[1] == x) & (dest[2] == s)

    def each_send(act):
        def over_rows(p):
            for dx in range(1, chan):
                dest = row_target(p, dx)
                index = zs * sub + p * (chan - 1) + dx - 1
                pl.when(jnp.logical_not(is_self(dest)))(
                    lambda: act(tile_copy(sub, dest, index))
                )

        def over_columns(dest_z):
            for ds in range(sub):
                dest = column_target(dest_z, ds)
                pl.when(jnp.logical_not(is_self(dest)))(
                    lambda: act(tile_copy(tile_slot, dest, dest_z * sub + ds))
                )

        farthest_first(over_columns)
        repeat(per_tile, over_rows)

    each_send(lambda copy: copy.start())

    row_tile = own_block // per_tile
    row_part = row_tile // sub
    row_place = jnp.where(row_part == x, row_tile % sub, sub)

    @pl.when(tile_part == x)
    def _():
        tiles[tile_slot, z] = layer_one

    @pl.when((row_tile == tile) & (row_part != x))
    def _():
        tiles[sub, z] = layer_one

    assemble(1)

    def tile_wait(place, source_tile, source_z):
        source = (source_z, source_tile % chan, source_tile // chan)

        @pl.when(jnp.logical_not(is_self(source)))
        def _():
            pltpu.make_async_remote_copy(
                src_ref=mine,
                dst_ref=tiles.at[place, source_z],
                send_sem=tile_send.at[0],
                recv_sem=tile_recv.at[place, source_z],
                device_id=device(*source),
                device_id_type=MESH,
            ).wait_recv()

    for q in range(sub):
        repeat(zs, lambda source_z: tile_wait(q, x * sub + q, source_z))

    @pl.when(row_part != x)
    def _():
        repeat(zs, lambda source_z: tile_wait(sub, row_tile, source_z))

    step_z = max(1, min(chunk_pixels // (chip_rows * width), zs))

    def edge_step(step):
        planes = pl.ds(step * step_z, step_z)
        values = tiles[row_place, planes].astype(jnp.float32)
        edges_one[planes] = gated(scaled_input(values, 1), 1, 0)

    repeat(zs // step_z, edge_step)

    row_offset = (own_block % per_tile) * block
    results = []
    for q in range(sub):

        def tri_step(step, totals):
            planes = pl.ds(step * step_z, step_z)
            values = tiles[q, planes].astype(jnp.float32)
            right = gated(scaled_input(values, 1), 1, 2)
            k_start = step * step_z * chip_rows
            if not isinstance(step, int):
                k_start = pl.multiple_of(k_start, chip_rows)
            mask_k = mask_cols[pl.ds(k_start, step_z * chip_rows)]
            right = right * mask_k.reshape(step_z, chip_rows, 1, -1)
            return tuple(
                total
                + jnp.sum(
                    right * edges_one[planes, :, pl.ds(row_offset + i, 1)], axis=(0, 1)
                )
                for i, total in enumerate(totals)
            )

        totals = tuple(jnp.zeros((width, in_gain.shape[-1]), jnp.float32) for _ in range(block))
        if zs // step_z == 1:
            totals = tri_step(0, totals)
        else:
            totals = lax.fori_loop(0, zs // step_z, tri_step, totals)
        start = pl.multiple_of((x * sub + q) * width, width)
        mask_j = mask_cols[pl.ds(start, width)]
        mask_i = [mask_cols[pl.ds(own_block * block + i, 1)] for i in range(block)]
        masked = jnp.stack([total * mask_j * m for total, m in zip(totals, mask_i)])
        own = tiles[q, z, pl.ds(s * block, block)].astype(jnp.float32)
        results.append(finish(masked, scaled_input(own, 1), own, 1))
    out_ref[...] = jnp.concatenate(results, axis=1).astype(out_ref.dtype)

    for ds in range(1, sub):
        left_copy(ds).wait_send()
    repeat(zs, lambda dz: pl.when(sends_right(dz))(lambda: right_copy(dz).wait_send()))
    for layer in range(2):
        for dx in range(1, chan):
            piece_copy(layer, dx).wait_send()
    each_send(lambda copy: copy.wait_send())


def shards(sizes, pair, residue_mask, in_gain, in_bias, projections, gate_weight, out_gain, out_bias, out_weight):
    zs, chan, sub = sizes
    block, length, channels = pair.shape
    projections = jnp.swapaxes(projections, 2, 3)
    layers, kinds, part, _ = projections.shape
    hidden = part * chan
    chip_rows = sub * block
    width = length // (chan * sub)
    per_tile = width // block
    f32, bf16 = jnp.float32, jnp.bfloat16
    dma = pltpu.SemaphoreType.DMA
    hbm = pl.BlockSpec(memory_space=pl.ANY)
    vmem = pl.BlockSpec(memory_space=pltpu.VMEM)
    return pl.pallas_call(
        functools.partial(kernel, (zs, chan, sub, block, length)),
        out_shape=jax.ShapeDtypeStruct((block, length // chan, channels), bf16),
        in_specs=[hbm, vmem] + [hbm] * 7,
        out_specs=vmem,
        scratch_shapes=[
            pltpu.VMEM((chip_rows, length, channels), bf16),
            pltpu.VMEM((width, length, channels), bf16),
            pltpu.VMEM((sub + 1, zs, chip_rows, width, channels), bf16),
            pltpu.VMEM((chip_rows, width, channels), bf16),
            pltpu.VMEM((layers, kinds, hidden, channels), bf16),
            pltpu.VMEM(in_gain.shape, f32),
            pltpu.VMEM(in_bias.shape, f32),
            pltpu.VMEM(gate_weight.shape, bf16),
            pltpu.VMEM(out_gain.shape, f32),
            pltpu.VMEM(out_bias.shape, f32),
            pltpu.VMEM(out_weight.shape, bf16),
            pltpu.VMEM((length, hidden), f32),
            pltpu.VMEM((chip_rows, length, channels), f32),
            pltpu.VMEM((chip_rows, length, channels), f32),
            pltpu.VMEM((chip_rows, length, hidden), f32),
            pltpu.VMEM((chip_rows, width, hidden), f32),
            pltpu.VMEM((zs, chip_rows, width, hidden), f32),
            dma((9,)),
            dma((zs + sub,)),
            dma((sub,)),
            dma((per_tile,)),
            dma((layers, chan)),
            dma((layers, chan)),
            dma((zs * sub + per_tile * chan,)),
            dma((sub + 1, zs)),
        ],
        compiler_params=pltpu.CompilerParams(
            collective_id=0, has_side_effects=True, vmem_limit_bytes=56 * 2**20
        ),
    )(
        pair,
        residue_mask.reshape(1, length),
        in_gain,
        in_bias,
        projections,
        gate_weight,
        out_gain,
        out_bias,
        out_weight,
    )


def solution(mesh):
    sizes = (mesh.shape["rows"], mesh.shape["chan"], mesh.shape["sub"])
    placed = (
        P(("crops", "rows", "sub"), None, None),
        P("crops"),
        P(),
        P(),
        P(None, None, None, "chan"),
        P(),
        P(),
        P(),
        P(),
    )
    return jax.shard_map(
        functools.partial(shards, sizes),
        mesh=mesh,
        in_specs=placed,
        out_specs=P(("crops", "rows", "sub"), "chan", None),
        check_vma=False,
    )
```

```python
import functools

import jax
import jax.numpy as jnp
from jax import lax
from jax.experimental import pallas as pl
from jax.experimental.pallas import tpu as pltpu
from jax.sharding import PartitionSpec as P

epsilon = 1e-05
chunk_pixels = 256
MESH = pl.DeviceIdType.MESH


def normalize(values):
    centre = jnp.mean(values, axis=-1, keepdims=True)
    centred = values - centre
    spread = jnp.mean(centred * centred, axis=-1, keepdims=True)
    return centred * lax.rsqrt(spread + epsilon)


def sigmoid(values):
    return 0.5 * jnp.tanh(0.5 * values) + 0.5


def matmul(values, weight):
    flat = values.astype(jnp.bfloat16).reshape(-1, values.shape[-1])
    out = jnp.dot(flat, weight, preferred_element_type=jnp.float32)
    return out.reshape(values.shape[:-1] + (weight.shape[-1],))


def matmul_transposed(values, weight):
    flat = values.astype(jnp.bfloat16).reshape(-1, values.shape[-1])
    out = lax.dot_general(
        flat, weight, (((1,), (1,)), ((), ())), preferred_element_type=jnp.float32
    )
    return out.reshape(values.shape[:-1] + (weight.shape[0],))


def repeat(count, body):
    if count <= 8:
        for step in range(count):
            body(step)
    else:
        lax.fori_loop(0, count, lambda step, _: (body(step), 0)[1], 0)


def kernel(
    sizes,
    pair_ref,
    mask_ref,
    in_gain_ref,
    in_bias_ref,
    proj_ref,
    gate_ref,
    out_gain_ref,
    out_bias_ref,
    weight_ref,
    out_ref,
    left_rows,
    right_rows,
    tiles,
    mine,
    full,
    in_gain,
    in_bias,
    gate,
    out_gain,
    out_bias,
    weight,
    mask_cols,
    residual,
    normed,
    edges,
    triangle,
    edges_one,
    local_sem,
    first_send,
    left_recv,
    right_recv,
    piece_send,
    piece_recv,
    tile_send,
    tile_recv,
):
    zs, chan, sub, block, length = sizes
    chip_rows = sub * block
    width = length // (chan * sub)
    per_tile = width // block
    z, x, s = lax.axis_index("rows"), lax.axis_index("chan"), lax.axis_index("sub")
    own_block = z * sub + s
    tile = s * chan + x
    tile_part, tile_slot = tile // sub, tile % sub

    def device(dz, dx, ds):
        return {"rows": dz, "chan": dx, "sub": ds}

    part = proj_ref.shape[2]
    own_part = pl.ds(pl.multiple_of(x * part, part), part)
    own_rows = left_rows.at[pl.ds(s * block, block)]

    def farthest_first(act):
        def at_distance(step):
            distance = zs - 1 - step
            pl.when(z + distance < zs)(lambda: act(z + distance))
            pl.when(z - distance >= 0)(lambda: act(z - distance))

        repeat(zs - 1, at_distance)
        act(z)

    barrier = pltpu.get_barrier_semaphore()
    others = chan * sub

    def greet(dest_z):
        for inner in range(others):
            dx, ds = inner // sub, inner % sub

            def signal():
                pl.semaphore_signal(
                    barrier,
                    inc=1,
                    device_id=device(dest_z, (x + dx) % chan, (s + ds) % sub),
                    device_id_type=MESH,
                )

            if inner == 0:
                pl.when(dest_z != z)(signal)
            else:
                signal()

    farthest_first(greet)
    small = [
        pltpu.make_async_copy(source, target, local_sem.at[index])
        for index, (source, target) in enumerate(
            (
                (pair_ref, own_rows),
                (proj_ref.at[0], full.at[0, :, own_part]),
                (proj_ref.at[1], full.at[1, :, own_part]),
                (in_gain_ref, in_gain),
                (in_bias_ref, in_bias),
                (gate_ref, gate),
                (out_gain_ref, out_gain),
                (out_bias_ref, out_bias),
                (weight_ref, weight),
            )
        )
    ]
    for copy in small:
        copy.start()

    rows_iota = lax.broadcasted_iota(jnp.int32, (length, length), 0)
    cols_iota = lax.broadcasted_iota(jnp.int32, (length, length), 1)
    mask_row = mask_ref[...].astype(jnp.float32)
    mask_col = jnp.sum(jnp.where(rows_iota == cols_iota, mask_row, 0.0), axis=1, keepdims=True)
    mask_cols[...] = jnp.broadcast_to(mask_col, mask_cols.shape)
    pl.semaphore_wait(barrier, zs * others - 1)

    for copy in small:
        copy.wait()

    target_tile = own_block // per_tile
    target_x, target_s = target_tile % chan, target_tile // chan
    slot = own_block % per_tile

    def left_copy(ds):
        return pltpu.make_async_remote_copy(
            src_ref=own_rows,
            dst_ref=left_rows.at[pl.ds(s * block, block)],
            send_sem=first_send.at[zs + ds - 1],
            recv_sem=left_recv.at[s],
            device_id=device(z, x, (s + ds) % sub),
            device_id_type=MESH,
        )

    def right_copy(dest_z):
        return pltpu.make_async_remote_copy(
            src_ref=own_rows,
            dst_ref=right_rows.at[pl.ds(slot * block, block)],
            send_sem=first_send.at[dest_z],
            recv_sem=right_recv.at[slot],
            device_id=device(dest_z, x, target_s),
            device_id_type=MESH,
        )

    def sends_right(dest_z):
        return (x == target_x) & ((dest_z != z) | (target_s != s))

    def piece_copy(layer, dx):
        return pltpu.make_async_remote_copy(
            src_ref=full.at[layer, :, own_part],
            dst_ref=full.at[layer, :, own_part],
            send_sem=piece_send.at[layer, dx - 1],
            recv_sem=piece_recv.at[layer, x],
            device_id=device(z, (x + dx) % chan, s),
            device_id_type=MESH,
        )

    def start_right(dest_z):
        pl.when(sends_right(dest_z))(lambda: right_copy(dest_z).start())

    farthest_first(start_right)
    for dx in range(1, chan):
        piece_copy(0, dx).start()
    for ds in range(1, sub):
        left_copy(ds).start()
    for dx in range(1, chan):
        piece_copy(1, dx).start()


    def assemble(layer):
        for other in range(1, chan):
            source = (x + other) % chan
            pltpu.make_async_remote_copy(
                src_ref=full.at[layer, :, own_part],
                dst_ref=full.at[layer, :, pl.ds(pl.multiple_of(source * part, part), part)],
                send_sem=piece_send.at[layer, other - 1],
                recv_sem=piece_recv.at[layer, source],
                device_id=device(z, source, s),
                device_id_type=MESH,
            ).wait_recv()

    def scaled_input(values, layer):
        return normalize(values) * in_gain[layer : layer + 1] + in_bias[layer : layer + 1]

    def gated(values, layer, q):
        gate_part = matmul_transposed(values, full[layer, q])
        return sigmoid(gate_part) * matmul_transposed(values, full[layer, q + 1])

    def finish(values, normed_part, residual_part, layer):
        whole = values.astype(jnp.bfloat16).astype(jnp.float32)
        scaled = normalize(whole) * out_gain[layer : layer + 1] + out_bias[layer : layer + 1]
        update = matmul(scaled, weight[layer])
        gating = sigmoid(matmul(normed_part, gate[layer]))
        return residual_part + gating * update

    for ds in range(1, sub):
        source = (s + ds) % sub
        pltpu.make_async_remote_copy(
            src_ref=own_rows,
            dst_ref=left_rows.at[pl.ds(source * block, block)],
            send_sem=first_send.at[zs + ds - 1],
            recv_sem=left_recv.at[source],
            device_id=device(z, x, source),
            device_id_type=MESH,
        ).wait_recv()
    assemble(0)

    step_rows = max(1, min(chunk_pixels // length, chip_rows, width))

    def left_step(step):
        rows = pl.ds(step * step_rows, step_rows)
        values = left_rows[rows].astype(jnp.float32)
        ready = scaled_input(values, 0)
        residual[rows] = values
        normed[rows] = ready
        edges[rows] = gated(ready, 0, 0)

    repeat(chip_rows // step_rows, left_step)

    def right_arrival(p):
        source = tile * per_tile + p
        where = pl.ds(p * block, block)

        @pl.when(source == own_block)
        def _():
            right_rows[where] = left_rows[pl.ds(s * block, block)]

        @pl.when(source != own_block)
        def _():
            pltpu.make_async_remote_copy(
                src_ref=own_rows,
                dst_ref=right_rows.at[where],
                send_sem=first_send.at[0],
                recv_sem=right_recv.at[p],
                device_id=device(source // sub, x, source % sub),
                device_id_type=MESH,
            ).wait_recv()

    repeat(per_tile, right_arrival)

    def right_step(step):
        rows = pl.ds(step * step_rows, step_rows)
        values = right_rows[rows].astype(jnp.float32)
        right = gated(scaled_input(values, 0), 0, 2) * mask_cols[...]

        def one(i):
            triangle[i, rows] = jnp.sum(right * edges[i], axis=1)

        repeat(chip_rows, one)

    repeat(width // step_rows, right_step)

    columns = pl.ds(pl.multiple_of(tile * width, width), width)
    mask_i = mask_cols[pl.ds(pl.multiple_of(z * chip_rows, chip_rows), chip_rows)]
    masked = triangle[...] * mask_cols[columns] * mask_i.reshape(chip_rows, 1, -1)
    layer_one = finish(masked, normed[:, columns], residual[:, columns], 0).astype(jnp.bfloat16)
    mine[...] = layer_one

    def tile_copy(place, dest, index):
        return pltpu.make_async_remote_copy(
            src_ref=mine,
            dst_ref=tiles.at[place, z],
            send_sem=tile_send.at[index],
            recv_sem=tile_recv.at[place, z],
            device_id=device(*dest),
            device_id_type=MESH,
        )

    def column_target(dest_z, ds):
        return (dest_z, tile_part, (s + ds) % sub)

    def row_target(p, dx):
        target = tile * per_tile + p
        return (target // sub, (tile_part + dx) % chan, target % sub)

    def is_self(dest):
        return (dest[0] == z) & (dest[1] == x) & (dest[2] == s)

    def each_send(act):
        def over_rows(p):
            for dx in range(1, chan):
                dest = row_target(p, dx)
                index = zs * sub + p * (chan - 1) + dx - 1
                pl.when(jnp.logical_not(is_self(dest)))(
                    lambda: act(tile_copy(sub, dest, index))
                )

        def over_columns(dest_z):
            for ds in range(sub):
                dest = column_target(dest_z, ds)
                pl.when(jnp.logical_not(is_self(dest)))(
                    lambda: act(tile_copy(tile_slot, dest, dest_z * sub + ds))
                )

        farthest_first(over_columns)
        repeat(per_tile, over_rows)

    each_send(lambda copy: copy.start())

    row_tile = own_block // per_tile
    row_part = row_tile // sub
    row_place = jnp.where(row_part == x, row_tile % sub, sub)

    @pl.when(tile_part == x)
    def _():
        tiles[tile_slot, z] = layer_one

    @pl.when((row_tile == tile) & (row_part != x))
    def _():
        tiles[sub, z] = layer_one

    assemble(1)

    def tile_wait(place, source_tile, source_z):
        source = (source_z, source_tile % chan, source_tile // chan)

        @pl.when(jnp.logical_not(is_self(source)))
        def _():
            pltpu.make_async_remote_copy(
                src_ref=mine,
                dst_ref=tiles.at[place, source_z],
                send_sem=tile_send.at[0],
                recv_sem=tile_recv.at[place, source_z],
                device_id=device(*source),
                device_id_type=MESH,
            ).wait_recv()

    for q in range(sub):
        repeat(zs, lambda source_z: tile_wait(q, x * sub + q, source_z))

    @pl.when(row_part != x)
    def _():
        repeat(zs, lambda source_z: tile_wait(sub, row_tile, source_z))

    step_z = max(1, min(chunk_pixels // (chip_rows * width), zs))

    def edge_step(step):
        planes = pl.ds(step * step_z, step_z)
        values = tiles[row_place, planes].astype(jnp.float32)
        edges_one[planes] = gated(scaled_input(values, 1), 1, 0)

    repeat(zs // step_z, edge_step)

    row_offset = (own_block % per_tile) * block
    results = []
    for q in range(sub):

        def tri_step(step, totals):
            planes = pl.ds(step * step_z, step_z)
            values = tiles[q, planes].astype(jnp.float32)
            right = gated(scaled_input(values, 1), 1, 2)
            k_start = step * step_z * chip_rows
            if not isinstance(step, int):
                k_start = pl.multiple_of(k_start, chip_rows)
            mask_k = mask_cols[pl.ds(k_start, step_z * chip_rows)]
            right = right * mask_k.reshape(step_z, chip_rows, 1, -1)
            return tuple(
                total
                + jnp.sum(
                    right * edges_one[planes, :, pl.ds(row_offset + i, 1)], axis=(0, 1)
                )
                for i, total in enumerate(totals)
            )

        totals = tuple(jnp.zeros((width, in_gain.shape[-1]), jnp.float32) for _ in range(block))
        if zs // step_z == 1:
            totals = tri_step(0, totals)
        else:
            totals = lax.fori_loop(0, zs // step_z, tri_step, totals)
        start = pl.multiple_of((x * sub + q) * width, width)
        mask_j = mask_cols[pl.ds(start, width)]
        mask_i = [mask_cols[pl.ds(own_block * block + i, 1)] for i in range(block)]
        masked = jnp.stack([total * mask_j * m for total, m in zip(totals, mask_i)])
        own = tiles[q, z, pl.ds(s * block, block)].astype(jnp.float32)
        results.append(finish(masked, scaled_input(own, 1), own, 1))
    out_ref[...] = jnp.concatenate(results, axis=1).astype(out_ref.dtype)

    for ds in range(1, sub):
        left_copy(ds).wait_send()
    repeat(zs, lambda dz: pl.when(sends_right(dz))(lambda: right_copy(dz).wait_send()))
    for layer in range(2):
        for dx in range(1, chan):
            piece_copy(layer, dx).wait_send()
    each_send(lambda copy: copy.wait_send())


def shards(sizes, pair, residue_mask, in_gain, in_bias, projections, gate_weight, out_gain, out_bias, out_weight):
    zs, chan, sub = sizes
    block, length, channels = pair.shape
    projections = jnp.swapaxes(projections, 2, 3)
    layers, kinds, part, _ = projections.shape
    hidden = part * chan
    chip_rows = sub * block
    width = length // (chan * sub)
    per_tile = width // block
    f32, bf16 = jnp.float32, jnp.bfloat16
    dma = pltpu.SemaphoreType.DMA
    hbm = pl.BlockSpec(memory_space=pl.ANY)
    vmem = pl.BlockSpec(memory_space=pltpu.VMEM)
    return pl.pallas_call(
        functools.partial(kernel, (zs, chan, sub, block, length)),
        out_shape=jax.ShapeDtypeStruct((block, length // chan, channels), bf16),
        in_specs=[hbm, vmem] + [hbm] * 7,
        out_specs=vmem,
        scratch_shapes=[
            pltpu.VMEM((chip_rows, length, channels), bf16),
            pltpu.VMEM((width, length, channels), bf16),
            pltpu.VMEM((sub + 1, zs, chip_rows, width, channels), bf16),
            pltpu.VMEM((chip_rows, width, channels), bf16),
            pltpu.VMEM((layers, kinds, hidden, channels), bf16),
            pltpu.VMEM(in_gain.shape, f32),
            pltpu.VMEM(in_bias.shape, f32),
            pltpu.VMEM(gate_weight.shape, bf16),
            pltpu.VMEM(out_gain.shape, f32),
            pltpu.VMEM(out_bias.shape, f32),
            pltpu.VMEM(out_weight.shape, bf16),
            pltpu.VMEM((length, hidden), f32),
            pltpu.VMEM((chip_rows, length, channels), f32),
            pltpu.VMEM((chip_rows, length, channels), f32),
            pltpu.VMEM((chip_rows, length, hidden), f32),
            pltpu.VMEM((chip_rows, width, hidden), f32),
            pltpu.VMEM((zs, chip_rows, width, hidden), f32),
            dma((9,)),
            dma((zs + sub,)),
            dma((sub,)),
            dma((per_tile,)),
            dma((layers, chan)),
            dma((layers, chan)),
            dma((zs * sub + per_tile * chan,)),
            dma((sub + 1, zs)),
        ],
        compiler_params=pltpu.CompilerParams(
            collective_id=0, has_side_effects=True, vmem_limit_bytes=56 * 2**20
        ),
    )(
        pair,
        residue_mask.reshape(1, length),
        in_gain,
        in_bias,
        projections,
        gate_weight,
        out_gain,
        out_bias,
        out_weight,
    )


def solution(mesh):
    sizes = (mesh.shape["rows"], mesh.shape["chan"], mesh.shape["sub"])
    placed = (
        P(("crops", "rows", "sub"), None, None),
        P("crops"),
        P(),
        P(),
        P(None, None, None, "chan"),
        P(),
        P(),
        P(),
        P(),
    )
    return jax.shard_map(
        functools.partial(shards, sizes),
        mesh=mesh,
        in_specs=placed,
        out_specs=P(("crops", "rows", "sub"), "chan", None),
        check_vma=False,
    )
```
